512 devices in a mesh: span: 64 (over x, z, core), elem: 8 (over y).
Axes of the slice: x: 4, y: 8, z: 8, core: 2. Of those that a mesh axis runs over, the one named last changes fastest.
Arguments:
- current_block: float32 [64, 64, 20480], P('span', None, 'elem'), may hold values from -6 to 6
- search_block: float32 [64, 64, 20480], P('span', None, 'elem'), may hold values from -6 to 6
- previous_block: float32 [64, 64, 20480], P('span', None, 'elem'), may hold values from -6 to 6
- ground_spring: float32 [20480], P('elem'), may hold values from 1 to 18
- wire_tension: float32 [20480], P('elem'), may hold values from 0.3 to 13.5
- dropper_stiff: float32 [20480], P('elem'), may hold values from 0.3 to 3
- dropper_offset: int32 [20480], P('elem'), may hold values from 1 to 8
- span_link: float32 [20480], P('elem'), may hold values from 0.1 to 0.4
- ritz_rotation: float32 [64, 192, 64], P('span'), may hold values from -0.4375 to 0.4375
Outputs:
- next_block: float32 [64, 64, 20480], P('span', None, 'elem')
- next_residual: float32 [64, 64, 20480], P('span', None, 'elem')
- ritz_values: float32 [64, 64], P('span')
The draws below stay inside these ranges and needn't reach their ends.
Inputs may be any that keep to these rules, and one draw needn't show every extreme that they name: `dropper_offset`: 20480 * i is joined by a dropper to 20480 * i + dropper_offset_i; droppers that would reach past 20480 20480 - 1 are absent.
All inputs are finite; a program needn't handle non-finite values.
Results may differ from the reference program's by a relative error of at most 0.00016.
Values sent between devices are 32-bit elements; how exact they have to be, the bound alone decides.
A program may use at most 128 MiB of HBM per device.

```python
import math
import jax
import jax.numpy as jnp
from jax import lax

DOF = 20480
M = 64
REACH = 8
SPANS = 64


def rising_draw(key, low, high):
    position = jnp.arange(DOF).astype(jnp.float32)
    rise = 3.0
    factor = jnp.exp(math.log(rise) * position / (DOF - 1))
    noise = jax.random.uniform(key, (DOF,), jnp.float32, low, high)
    return noise * factor


def draw_ground_spring(key, part):
    return rising_draw(jax.random.fold_in(key, 11), 1.0, 2.0)


def draw_wire_tension(key, part):
    return rising_draw(jax.random.fold_in(key, 23), 0.3, 1.5)


def set_ends(array, stream_key, least, largest):
    longest = array.shape.index(max(array.shape))
    spots = []
    for shift in (0, 1):
        where = [jax.random.randint(jax.random.fold_in(stream_key, axis), (), 0, length) for axis, length in enumerate(array.shape)]
        where[longest] = (where[longest] + shift) % array.shape[longest]
        spots.append(tuple(where))
    return array.at[spots[0]].set(least).at[spots[1]].set(largest)


def block_levels(stream_key, dims, split, least, largest):
    def one(axis_at, shards_of):
        draws = jax.random.uniform(jax.random.fold_in(jax.random.fold_in(stream_key, 6), axis_at), (shards_of,), jnp.float32, least / len(split), largest / len(split))
        return jnp.repeat(jnp.exp(draws), dims[axis_at] // shards_of).reshape((-1,) + (1,) * (len(dims) - axis_at - 1))

    gain = one(*split[0])
    for cut in split[1:]:
        gain = gain * one(*cut)
    return gain


def bell_draw(stream_key, extent, scale, most, split=(), dtype=jnp.bfloat16):
    array = scale * jax.random.normal(stream_key, extent, jnp.float32)
    if split:
        array = array * block_levels(stream_key, extent, split, -0.22, 0.18)
    return jnp.clip(array, -most, most).astype(dtype)


def setup_inputs(seed: int = 0) -> dict:
    streams_of = jax.random.split(jax.random.key(seed), 10)
    current_block = bell_draw(streams_of[0], (SPANS, M, DOF), 1.0, 6.0, ((0, 64), (2, 8)), jnp.float32)
    search_block = bell_draw(streams_of[1], (SPANS, M, DOF), 1.0, 6.0, ((0, 64), (2, 8)), jnp.float32)
    previous_block = bell_draw(streams_of[2], (SPANS, M, DOF), 1.0, 6.0, ((0, 64), (2, 8)), jnp.float32)
    ground_spring = draw_ground_spring(jax.random.fold_in(streams_of[9], 71), 0)
    wire_tension = draw_wire_tension(jax.random.fold_in(streams_of[9], 71), 0)
    dropper_stiff = jnp.clip(jnp.exp(math.log(3.0) - 2.3025851 * jax.random.uniform(streams_of[5], (DOF,), jnp.float32) ** block_levels(streams_of[5], (DOF,), ((0, 8),), -0.2, 0.2)), 0.3, 3.0)
    dropper_offset = set_ends(jax.random.randint(streams_of[6], (DOF,), 1, REACH + 1), jax.random.fold_in(streams_of[6], 1), 1, REACH).astype(jnp.int32)
    span_link = jnp.clip(0.1 + 0.3 * jax.random.uniform(streams_of[7], (DOF,), jnp.float32) ** block_levels(streams_of[7], (DOF,), ((0, 8),), -0.2, 0.2), 0.1, 0.4)
    ritz_rotation = bell_draw(streams_of[8], (SPANS, 3 * M, M), (3 * M) ** -0.5, 0.4375, ((0, 64),), jnp.float32)
    return dict(current_block=current_block, search_block=search_block, previous_block=previous_block, ground_spring=ground_spring, wire_tension=wire_tension, dropper_stiff=dropper_stiff, dropper_offset=dropper_offset, span_link=span_link, ritz_rotation=ritz_rotation)


def fourier_rows(count):
    row = jnp.arange(count)[:, None]
    col = jnp.arange(count)[None, :]
    half = count // 2
    wave = jnp.where(row <= half, row, row - half)
    phase = (wave * col % count).astype(jnp.float32) * (2.0 * math.pi / count)
    scaled = jnp.where(row <= half, jnp.cos(phase), jnp.sin(phase)) * math.sqrt(2.0 / count)
    edge = (row == 0) | (row == half)
    matrix = jnp.where(edge, jnp.cos(phase) * math.sqrt(1.0 / count), scaled)
    slots = jnp.arange(count)
    slot_wave = jnp.where(slots <= half, slots, slots - half)
    cosines = jnp.cos(slot_wave.astype(jnp.float32) * (2.0 * math.pi / count))
    return (matrix, cosines)

def along_spans(matrix, block):
    shape = block.shape
    flat = block.reshape(shape[0], -1)
    return jnp.dot(matrix, flat, precision=lax.Precision.HIGHEST).reshape(shape)

def shift_up(field, distance):
    return jnp.concatenate([field[:, distance:], jnp.zeros_like(field[:, :distance])], 1)

def shift_down(field, distance):
    return jnp.concatenate([jnp.zeros_like(field[:, :distance]), field[:, :-distance]], 1)

def apply_span(field, ground, tension, dropper_rows, link_term):
    flux = tension * (field - shift_up(field, 1))
    applied = ground * field + flux - shift_down(flux, 1)
    for distance in range(1, REACH + 1):
        flux = dropper_rows[distance - 1] * (field - shift_up(field, distance))
        applied = applied + flux - shift_down(flux, distance)
    return applied + link_term * field

def reference(current_block, search_block, previous_block, ground_spring, wire_tension, dropper_stiff, dropper_offset, span_link, ritz_rotation):
    matrix, cosines = fourier_rows(SPANS)
    position = jnp.arange(DOF).astype(jnp.int32)
    tension = jnp.where(position < DOF - 1, wire_tension, jnp.zeros_like(wire_tension))
    dropper_rows = jnp.stack([jnp.where((dropper_offset == distance) & (position + distance < DOF), dropper_stiff, jnp.zeros_like(dropper_stiff)) for distance in range(1, REACH + 1)])
    link_terms = 2.0 * (1.0 - cosines)
    slot_x = along_spans(matrix, current_block)
    slot_w = along_spans(matrix, search_block)
    slot_p = along_spans(matrix, previous_block)

    def one_slot(items):
        field_x, field_w, field_p, rotation, link_term = items
        stacked = jnp.concatenate([field_x, field_w, field_p], 0)
        applied = apply_span(stacked, ground_spring, tension, dropper_rows, link_term * span_link)
        projected = jnp.dot(rotation.T, stacked, precision=lax.Precision.HIGHEST)
        stiff_projected = jnp.dot(rotation.T, applied, precision=lax.Precision.HIGHEST)
        energy = lax.optimization_barrier(jnp.sum(projected * stiff_projected, axis=1))
        weight_sum = lax.optimization_barrier(jnp.sum(projected * projected, axis=1))
        ritz = energy / (weight_sum + 1e-06)
        residual = stiff_projected - ritz[:, None] * projected
        return (projected, residual, ritz)
    projected, residual, ritz = lax.map(one_slot, (slot_x, slot_w, slot_p, ritz_rotation, link_terms))
    return (along_spans(matrix.T, projected), along_spans(matrix.T, residual), ritz)
```

```python
import functools
import math

import jax
import jax.numpy as jnp
import ml_dtypes
import numpy as np
from jax import lax
from jax.experimental import pallas as pl
from jax.experimental.pallas import tpu as pltpu
from jax.sharding import PartitionSpec as P

REACH = 8
SPANS = 64
M = 64
HALF = 20
PAD = 24
LANES = 128
F32 = jnp.float32
BF16 = jnp.bfloat16
VMEM = pltpu.VMEM


def split_np(matrix):
    high = matrix.astype(np.float32).astype(ml_dtypes.bfloat16)
    low = (matrix - high.astype(np.float64)).astype(ml_dtypes.bfloat16)
    return high, low


def fourier_np(count):
    half = count // 2
    row = np.arange(count)[:, None]
    col = np.arange(count)[None, :]
    wave = np.where(row <= half, row, row - half)
    phase = (wave * col % count) * (2.0 * math.pi / count)
    scaled = np.where(row <= half, np.cos(phase), np.sin(phase)) * math.sqrt(2.0 / count)
    edge = (row == 0) | (row == half)
    matrix = np.where(edge, np.cos(phase) * math.sqrt(1.0 / count), scaled)
    slots = np.arange(count)
    slot_wave = np.where(slots <= half, slots, slots - half)
    links = 2.0 * (1.0 - np.cos(slot_wave * (2.0 * math.pi / count)))
    return matrix, links


def left_terms(matrix):
    high, low = split_np(matrix)
    return np.concatenate([high, low, high], 1)


def split(value):
    high = value.astype(BF16)
    low = (value - high.astype(F32)).astype(BF16)
    return high, low


def right_rows(value):
    high, low = split(value)
    return jnp.concatenate([high, high, low], 0)


def lane_low(shape):
    return lax.broadcasted_iota(jnp.int32, shape, len(shape) - 1) < M


def full(count):
    return [pl.BlockSpec(memory_space=VMEM)] * count


def params(collective=None, limit=56):
    return pltpu.CompilerParams(
        vmem_limit_bytes=limit << 20,
        collective_id=collective,
        has_side_effects=collective is not None,
    )


def pack_kernel(x_ref, w_ref, p_ref, xw_ref, pp_ref):
    dofs = x_ref.shape[1]
    p = p_ref[...]
    moved = pltpu.roll(p, dofs - HALF, 1)
    for block in range(dofs // LANES):
        at = slice(block * LANES, (block + 1) * LANES)
        xw_ref[at, :] = jnp.concatenate([x_ref[:, at], w_ref[:, at]], 0).T
        pp_ref[at, :] = jnp.concatenate([p[:, at], moved[:, at]], 0).T


def arrived(ref, sem):
    pltpu.make_async_copy(ref, ref, sem).wait()


def greet(spans):
    me = lax.axis_index("span")
    barrier = pltpu.get_barrier_semaphore()

    def signal(step, _):
        pl.semaphore_signal(
            barrier,
            inc=1,
            device_id={"span": lax.rem(me + step, spans)},
            device_id_type=pl.DeviceIdType.MESH,
        )
        return 0

    lax.fori_loop(1, spans, signal, 0)
    return barrier


def send(src, dst, send_sem, recv_sem, device):
    copy = pltpu.make_async_remote_copy(
        src_ref=src,
        dst_ref=dst,
        send_sem=send_sem,
        recv_sem=recv_sem,
        device_id=device,
        device_id_type=pl.DeviceIdType.MESH,
    )
    copy.start()
    return copy


def forward_kernel(xw_ref, pp_ref, rot_ref, edge_ref, rxw_ref, rpp_ref, rall_ref, left_ref, sems, rsems):
    spans = SPANS
    me = lax.axis_index("span")
    ex, count_x = me // 16, 4
    ez, count_z = lax.rem(me // 2, 8), 8
    ec = lax.rem(me, 2)
    elem = lax.axis_index("elem")
    elems = lax.axis_size("elem")
    barrier = greet(spans)
    after, before = lax.rem(elem + 1, elems), lax.rem(elem + elems - 1, elems)
    for other in (after, before):
        pl.semaphore_signal(
            barrier, inc=1, device_id={"elem": other}, device_id_type=pl.DeviceIdType.MESH
        )
    own = [
        pltpu.make_async_copy(rot_ref, rall_ref.at[ex, ez, ec], rsems.at[8]),
        pltpu.make_async_copy(xw_ref.at[me], rxw_ref.at[:, me], rsems.at[9]),
        pltpu.make_async_copy(pp_ref.at[2 * me], rpp_ref.at[:, me], rsems.at[10]),
    ]
    for copy in own:
        copy.start()
    pl.semaphore_wait(barrier, spans - 1 + 2)

    def at(x, z, c):
        return {"span": (x * 8 + z) * 2 + c}

    for step in range(1, count_z):
        send(
            rot_ref,
            rall_ref.at[ex, ez, ec],
            rsems.at[0],
            rsems.at[1],
            at(ex, lax.rem(ez + step, count_z), ec),
        )
    edge = send(edge_ref, left_ref, rsems.at[6], rsems.at[7], {"elem": after})

    def body(step, _):
        other = lax.rem(me + step, spans)
        send(xw_ref.at[other], rxw_ref.at[:, me], sems.at[0], sems.at[1], {"span": other})
        send(pp_ref.at[2 * other], rpp_ref.at[:, me], sems.at[2], sems.at[3], {"span": other})
        return 0

    lax.fori_loop(1, spans, body, 0)
    own[0].wait()
    arrived(rall_ref.at[0, pl.ds(0, count_z - 1), 0], rsems.at[1])
    for step in range(1, count_x):
        send(
            rall_ref.at[ex, :, ec],
            rall_ref.at[ex, :, ec],
            rsems.at[2],
            rsems.at[3],
            at(lax.rem(ex + step, count_x), ez, ec),
        )
    arrived(rall_ref.at[pl.ds(0, count_x - 1), :, 0], rsems.at[3])
    cross = send(
        rall_ref.at[:, :, ec], rall_ref.at[:, :, ec], rsems.at[4], rsems.at[5], at(ex, ez, 1 - ec)
    )
    arrived(rall_ref.at[0, pl.ds(0, count_z - 1), 0], rsems.at[0])
    arrived(rall_ref.at[pl.ds(0, count_x - 1), :, 0], rsems.at[2])
    cross.wait()
    edge.wait()
    own[1].wait()
    own[2].wait()
    arrived(rxw_ref.at[:, pl.ds(0, spans - 1)], sems.at[0])
    arrived(rxw_ref.at[:, pl.ds(0, spans - 1)], sems.at[1])
    arrived(rpp_ref.at[:, pl.ds(0, spans - 1)], sems.at[2])
    arrived(rpp_ref.at[:, pl.ds(0, spans - 1)], sems.at[3])


def rotate_kernel(xw_ref, pp_ref, rall_ref, four_ref, out_ref, low_ref, high_ref, slot_ref):
    slot_ref[...] = jnp.zeros_like(slot_ref)
    group = 4

    def transform(source, base, which, start):
        rows = jnp.concatenate([source[base + q] for q in range(group)], 1)
        moved = jnp.dot(four_ref[...], right_rows(rows), preferred_element_type=F32)
        for q in range(group):
            slot_ref[which, pl.ds(start + q, SPANS, stride=PAD), :] = moved[
                :, q * LANES : (q + 1) * LANES
            ]

    def chunk(step, _):
        at = step * group
        transform(xw_ref, at, 0, at)
        transform(xw_ref, at + HALF, 1, at)
        transform(pp_ref, at, 2, at)
        return 0

    lax.fori_loop(0, HALF // group, chunk, 0)
    low = lane_low((96, LANES))

    def slot(j, _):
        at = pl.ds(pl.multiple_of(j * PAD, 8), PAD)
        rows = jnp.concatenate([slot_ref[which, at, :] for which in range(3)], 1)
        high, rest = split(rows)
        left = jnp.concatenate([high, rest, high], 1)
        packed = rall_ref[j]
        turned = pltpu.roll(packed, M, 1)
        a_low, b_low = jnp.where(low, packed, 0.0), jnp.where(low, turned, 0.0)
        a_high, b_high = jnp.where(low, 0.0, turned), jnp.where(low, 0.0, packed)
        right = jnp.concatenate(
            [a_low, b_low[:32], a_high, b_high[:32], b_low[32:], b_high[32:]], 0
        )
        moved = jnp.dot(left, right_rows(right), preferred_element_type=F32)
        out_ref[at, :] = moved
        low_ref[j] = moved[:REACH]
        high_ref[j] = moved[HALF - REACH : HALF]
        return 0

    lax.fori_loop(0, SPANS, slot, 0)


def halo_kernel(low_ref, high_ref, left_ref, right_ref, sems):
    me, elem = lax.axis_index("span"), lax.axis_index("elem")
    spans, elems = lax.axis_size("span"), lax.axis_size("elem")
    up, down = me + 1, me + spans - 1
    after = {"span": lax.rem(up, spans), "elem": lax.rem(elem + up // spans, elems)}
    before = {
        "span": lax.rem(down, spans),
        "elem": lax.rem(elem + elems - 1 + down // spans, elems),
    }
    barrier = pltpu.get_barrier_semaphore()
    for other in (after, before):
        pl.semaphore_signal(barrier, inc=1, device_id=other, device_id_type=pl.DeviceIdType.MESH)
    pl.semaphore_wait(barrier, 2)
    copies = [
        send(high_ref, left_ref, sems.at[0], sems.at[1], after),
        send(low_ref, right_ref, sems.at[2], sems.at[3], before),
    ]
    for copy in copies:
        copy.wait()


def stiff_kernel(p_ref, low_ref, high_ref, left_ref, right_ref, band_ref, link_ref, slots_ref, out_ref, sums_ref):
    group = 4
    half = lane_low((REACH, LANES))
    low = lane_low((PAD, LANES))
    kept = lax.broadcasted_iota(jnp.int32, (PAD, LANES), 0) < HALF
    side = lane_low((1, LANES))
    high, rest = split(band_ref[...])
    band = jnp.concatenate([high, rest, high], 1)

    def body(step, _):
        pieces = []
        for q in range(group):
            j = step * group + q
            rows = p_ref[pl.ds(pl.multiple_of(j * PAD, 8), PAD), :]
            top = pltpu.roll(jnp.where(half, high_ref[j], left_ref[j]), M, 1)
            bottom = pltpu.roll(jnp.where(half, right_ref[j], low_ref[j]), M, 1)
            pieces.append(jnp.concatenate([rows, top, bottom], 0))
        wide = jnp.concatenate(pieces, 1)
        moved = jnp.dot(band, right_rows(wide), preferred_element_type=F32)
        for q in range(group):
            j = step * group + q
            at = slice(q * LANES, (q + 1) * LANES)
            rows = pieces[q][:PAD]
            stiff = jnp.where(low, moved[:PAD, at], moved[PAD:, at])
            stiff = stiff + slots_ref[j] * link_ref[...] * rows
            out_ref[pl.ds(pl.multiple_of(j * PAD, 8), PAD), :] = stiff
            energy = jnp.sum(jnp.where(kept, rows * stiff, 0.0), 0, keepdims=True)
            weight = jnp.sum(jnp.where(kept, rows * rows, 0.0), 0, keepdims=True)
            energy = energy + pltpu.roll(energy, M, 1)
            weight = weight + pltpu.roll(weight, M, 1)
            sums_ref[j] = jnp.where(side, energy, weight)
        return 0

    lax.fori_loop(0, SPANS // group, body, 0)


def ritz_kernel(sums_ref, all_ref, parts_ref, mine_ref, elems_ref, sems):
    spans, elems = SPANS, lax.axis_size("elem")
    me, elem = lax.axis_index("span"), lax.axis_index("elem")
    barrier = greet(spans)
    for step in range(1, elems):
        pl.semaphore_signal(
            barrier,
            inc=1,
            device_id={"elem": lax.rem(elem + step, elems)},
            device_id_type=pl.DeviceIdType.MESH,
        )
    parts_ref[me] = sums_ref[me]
    pl.semaphore_wait(barrier, spans - 1 + elems - 1)

    def scatter(step, _):
        other = lax.rem(me + step, spans)
        send(sums_ref.at[other], parts_ref.at[me], sems.at[0], sems.at[1], {"span": other})
        return 0

    lax.fori_loop(1, spans, scatter, 0)
    arrived(parts_ref.at[pl.ds(0, spans - 1)], sems.at[1])
    mine = jnp.sum(parts_ref[...], 0)
    mine_ref[...] = mine
    elems_ref[elem] = mine
    for step in range(1, elems):
        send(
            mine_ref,
            elems_ref.at[elem],
            sems.at[2],
            sems.at[3],
            {"elem": lax.rem(elem + step, elems)},
        )
    arrived(elems_ref.at[pl.ds(0, elems - 1)], sems.at[3])
    total = jnp.sum(elems_ref[...], 0)
    ritz = total / (pltpu.roll(total, M, 1) + 1e-06)
    ritz = jnp.where(lane_low((1, LANES)), ritz, pltpu.roll(ritz, M, 1))
    all_ref[me] = ritz

    def spread(step, _):
        other = lax.rem(me + step, spans)
        send(all_ref.at[me], all_ref.at[me], sems.at[4], sems.at[5], {"span": other})
        return 0

    lax.fori_loop(1, spans, spread, 0)
    arrived(parts_ref.at[pl.ds(0, spans - 1)], sems.at[0])
    arrived(elems_ref.at[pl.ds(0, elems - 1)], sems.at[2])
    arrived(all_ref.at[pl.ds(0, spans - 1)], sems.at[4])
    arrived(all_ref.at[pl.ds(0, spans - 1)], sems.at[5])


def return_kernel(p_ref, stiff_ref, ritz_ref, four_ref, block_ref, res_ref):
    group = 2

    def body(step, _):
        pieces = []
        for q in range(group):
            rows = pl.ds(step * group + q, SPANS, stride=PAD)
            projected = p_ref[rows, :]
            pieces += [projected, stiff_ref[rows, :] - ritz_ref[...] * projected]
        moved = jnp.dot(
            four_ref[...], right_rows(jnp.concatenate(pieces, 1)), preferred_element_type=F32
        )
        for q in range(group):
            k = step * group + q
            block_ref[k] = moved[:, 2 * q * LANES : (2 * q + 1) * LANES]
            res_ref[k] = moved[:, (2 * q + 1) * LANES : (2 * q + 2) * LANES]
        return 0

    lax.fori_loop(0, HALF // group, body, 0)


def backward_kernel(block_ref, res_ref, got_block_ref, got_res_ref, sems):
    spans = SPANS
    me = lax.axis_index("span")
    barrier = greet(spans)
    own = [
        pltpu.make_async_copy(block_ref.at[:, me], got_block_ref.at[me], sems.at[4]),
        pltpu.make_async_copy(res_ref.at[:, me], got_res_ref.at[me], sems.at[5]),
    ]
    for copy in own:
        copy.start()
    pl.semaphore_wait(barrier, spans - 1)

    def body(step, _):
        other = lax.rem(me + step, spans)
        where = {"span": other}
        send(block_ref.at[:, other], got_block_ref.at[me], sems.at[0], sems.at[1], where)
        send(res_ref.at[:, other], got_res_ref.at[me], sems.at[2], sems.at[3], where)
        return 0

    lax.fori_loop(1, spans, body, 0)
    for copy in own:
        copy.wait()
    arrived(got_block_ref.at[pl.ds(0, spans - 1)], sems.at[0])
    arrived(got_block_ref.at[pl.ds(0, spans - 1)], sems.at[1])
    arrived(got_res_ref.at[pl.ds(0, spans - 1)], sems.at[2])
    arrived(got_res_ref.at[pl.ds(0, spans - 1)], sems.at[3])


def unpack_kernel(block_ref, res_ref, next_ref, out_ref, rows_ref):
    low = lane_low((HALF, LANES))

    def body(i, _):
        block, res = block_ref[i], res_ref[i]
        first = jnp.where(low, block, pltpu.roll(res, M, 1))
        second = jnp.where(low, pltpu.roll(block, M, 1), res)
        rows_ref[pl.ds(pl.multiple_of(i * 2 * HALF, 8), 2 * HALF), :] = jnp.concatenate(
            [first, second], 0
        )
        return 0

    lax.fori_loop(0, SPANS, body, 0)
    for block in range(rows_ref.shape[0] // LANES):
        at = slice(block * LANES, (block + 1) * LANES)
        turned = rows_ref[at, :].T
        next_ref[:, at] = turned[:M]
        out_ref[:, at] = turned[M:]


def shape(*dims):
    return jax.ShapeDtypeStruct(dims, F32)


def band_terms(window, left, first):
    size = 2 * HALF + 2 * REACH
    lane = jnp.arange(size)
    window = jnp.where(first & (lane < REACH), left, window)
    ground, tension, dropper, offset = window[0], window[1], window[2], window[3]
    row, col = lane[:, None], lane[None, :]
    weight = jnp.where(col == row + 1, tension[:, None], 0.0)
    weight = weight + jnp.where(
        col == row + offset.astype(jnp.int32)[:, None], dropper[:, None], 0.0
    )
    both = weight + weight.T
    stiff = jnp.where(row == col, (ground + jnp.sum(both, 1))[:, None], 0.0) - both
    blank = jnp.zeros((HALF, PAD - HALF), F32)
    gap = jnp.zeros((PAD - HALF, PAD + 2 * REACH), F32)
    low, mid, high = REACH, REACH + HALF, REACH + 2 * HALF
    near, far = stiff[low:mid], stiff[mid:high]
    near = jnp.concatenate(
        [near[:, low:mid], blank, near[:, :low], near[:, mid : mid + REACH]], 1
    )
    far = jnp.concatenate([far[:, mid:high], blank, far[:, mid - REACH : mid], far[:, high:]], 1)
    return jnp.concatenate([near, gap, far, gap], 0)


def on_device(
    current_block,
    search_block,
    previous_block,
    ground_spring,
    wire_tension,
    dropper_stiff,
    dropper_offset,
    span_link,
    ritz_rotation,
):
    dofs = current_block.shape[2]
    spans, elems = lax.axis_size("span"), lax.axis_size("elem")
    me, elem = lax.axis_index("span"), lax.axis_index("elem")
    share = dofs // spans
    matrix, links = fourier_np(spans)

    position = elem * dofs + jnp.arange(dofs)
    total = dofs * elems
    tension = jnp.where(position < total - 1, wire_tension, 0.0)
    dropper = jnp.where(position + dropper_offset < total, dropper_stiff, 0.0)
    coefs = jnp.stack([ground_spring, tension, dropper, dropper_offset.astype(F32), span_link])
    edge = jnp.zeros((8, LANES), F32).at[:5, :REACH].set(coefs[:, dofs - REACH :])
    window = lax.dynamic_slice(
        jnp.pad(coefs, ((0, 0), (REACH, REACH))), (0, me * share), (5, share + 2 * REACH)
    )

    xw, pp = pl.pallas_call(
        pack_kernel,
        out_shape=(shape(dofs, LANES), shape(dofs, LANES)),
        in_specs=full(3),
        out_specs=tuple(full(2)),
        compiler_params=params(),
    )(current_block[0], search_block[0], previous_block[0])
    rotation = jnp.concatenate([ritz_rotation[0, :96], ritz_rotation[0, 96:]], 1)

    got_xw, got_pp, rotations, left_edge = pl.pallas_call(
        forward_kernel,
        out_shape=(
            shape(share, spans, 1, LANES),
            shape(HALF, spans, 1, LANES),
            shape(4, 8, 2, 96, LANES),
            shape(8, LANES),
        ),
        in_specs=full(4),
        out_specs=tuple(full(4)),
        scratch_shapes=[pltpu.SemaphoreType.DMA((4,)), pltpu.SemaphoreType.DMA((11,))],
        compiler_params=params(0),
    )(
        xw.reshape(spans, share, 1, LANES),
        pp.reshape(2 * spans, HALF, 1, LANES),
        rotation,
        edge,
    )

    rows = spans * PAD
    projected, low_edge, high_edge = pl.pallas_call(
        rotate_kernel,
        out_shape=(shape(rows, LANES), shape(spans, REACH, LANES), shape(spans, REACH, LANES)),
        in_specs=full(4),
        out_specs=tuple(full(3)),
        scratch_shapes=[pltpu.VMEM((3, rows, LANES), F32)],
        compiler_params=params(),
    )(
        got_xw.reshape(share, spans, LANES),
        got_pp.reshape(HALF, spans, LANES),
        rotations.reshape(spans, 96, LANES),
        jnp.asarray(left_terms(matrix)),
    )

    from_left, from_right = pl.pallas_call(
        halo_kernel,
        out_shape=(shape(spans, REACH, LANES), shape(spans, REACH, LANES)),
        in_specs=full(2),
        out_specs=tuple(full(2)),
        scratch_shapes=[pltpu.SemaphoreType.DMA((4,))],
        compiler_params=params(1),
    )(low_edge, high_edge)

    band = band_terms(window, jnp.pad(left_edge[:5, :REACH], ((0, 0), (0, share + REACH))), me == 0)
    link = window[4, REACH : REACH + share].reshape(2, HALF).T
    link = jnp.pad(jnp.repeat(link, M, 1), ((0, PAD - HALF), (0, 0)))
    slots = jnp.asarray(np.repeat(links[:, None, None], LANES, 2).astype(np.float32))
    stiff, sums = pl.pallas_call(
        stiff_kernel,
        out_shape=(shape(rows, LANES), shape(spans, 1, LANES)),
        in_specs=full(8),
        out_specs=tuple(full(2)),
        compiler_params=params(),
    )(projected, low_edge, high_edge, from_left, from_right, band, link, slots)

    ritz = pl.pallas_call(
        ritz_kernel,
        out_shape=shape(spans, 1, LANES),
        in_specs=full(1),
        out_specs=full(1)[0],
        scratch_shapes=[
            pltpu.VMEM((spans, 1, LANES), F32),
            pltpu.VMEM((1, LANES), F32),
            pltpu.VMEM((elems, 1, LANES), F32),
            pltpu.SemaphoreType.DMA((6,)),
        ],
        compiler_params=params(2),
    )(sums)

    block, res = pl.pallas_call(
        return_kernel,
        out_shape=(shape(HALF, spans, LANES), shape(HALF, spans, LANES)),
        in_specs=full(4),
        out_specs=tuple(full(2)),
        compiler_params=params(),
    )(projected, stiff, ritz.reshape(spans, LANES), jnp.asarray(left_terms(matrix.T)))

    got_block, got_res = pl.pallas_call(
        backward_kernel,
        out_shape=(shape(spans, HALF, 1, LANES), shape(spans, HALF, 1, LANES)),
        in_specs=full(2),
        out_specs=tuple(full(2)),
        scratch_shapes=[pltpu.SemaphoreType.DMA((6,))],
        compiler_params=params(3),
    )(block.reshape(HALF, spans, 1, LANES), res.reshape(HALF, spans, 1, LANES))

    next_block, next_residual = pl.pallas_call(
        unpack_kernel,
        out_shape=(shape(M, dofs), shape(M, dofs)),
        in_specs=full(2),
        out_specs=tuple(full(2)),
        scratch_shapes=[pltpu.VMEM((dofs, LANES), F32)],
        compiler_params=params(),
    )(got_block.reshape(spans, HALF, LANES), got_res.reshape(spans, HALF, LANES))
    mine = lax.dynamic_slice(ritz, (me, 0, 0), (1, 1, M)).reshape(1, M)
    return (next_block[None], next_residual[None], mine)


def solution(mesh):
    return jax.shard_map(
        on_device,
        mesh=mesh,
        in_specs=(
            P("span", None, "elem"),
            P("span", None, "elem"),
            P("span", None, "elem"),
            P("elem"),
            P("elem"),
            P("elem"),
            P("elem"),
            P("elem"),
            P("span", None, None),
        ),
        out_specs=(P("span", None, "elem"), P("span", None, "elem"), P("span", None)),
        check_vma=False,
    )
```

```python
import functools
import math

import jax
import jax.numpy as jnp
import ml_dtypes
import numpy as np
from jax import lax
from jax.experimental import pallas as pl
from jax.experimental.pallas import tpu as pltpu
from jax.sharding import PartitionSpec as P

REACH = 8
SPANS = 64
M = 64
HALF = 20
PAD = 24
LANES = 128
F32 = jnp.float32
BF16 = jnp.bfloat16
VMEM = pltpu.VMEM


def split_np(matrix):
    high = matrix.astype(np.float32).astype(ml_dtypes.bfloat16)
    low = (matrix - high.astype(np.float64)).astype(ml_dtypes.bfloat16)
    return high, low


def fourier_np(count):
    half = count // 2
    row = np.arange(count)[:, None]
    col = np.arange(count)[None, :]
    wave = np.where(row <= half, row, row - half)
    phase = (wave * col % count) * (2.0 * math.pi / count)
    scaled = np.where(row <= half, np.cos(phase), np.sin(phase)) * math.sqrt(2.0 / count)
    edge = (row == 0) | (row == half)
    matrix = np.where(edge, np.cos(phase) * math.sqrt(1.0 / count), scaled)
    slots = np.arange(count)
    slot_wave = np.where(slots <= half, slots, slots - half)
    links = 2.0 * (1.0 - np.cos(slot_wave * (2.0 * math.pi / count)))
    return matrix, links


def left_terms(matrix):
    high, low = split_np(matrix)
    return np.concatenate([high, low, high], 1)


def split(value):
    high = value.astype(BF16)
    low = (value - high.astype(F32)).astype(BF16)
    return high, low


def right_rows(value):
    high, low = split(value)
    return jnp.concatenate([high, high, low], 0)


def lane_low(shape):
    return lax.broadcasted_iota(jnp.int32, shape, len(shape) - 1) < M


def full(count):
    return [pl.BlockSpec(memory_space=VMEM)] * count


def params(collective=None, limit=56):
    return pltpu.CompilerParams(
        vmem_limit_bytes=limit << 20,
        collective_id=collective,
        has_side_effects=collective is not None,
    )


def arrived(ref, sem):
    pltpu.make_async_copy(ref, ref, sem).wait()


def send(src, dst, send_sem, recv_sem, device):
    copy = pltpu.make_async_remote_copy(
        src_ref=src,
        dst_ref=dst,
        send_sem=send_sem,
        recv_sem=recv_sem,
        device_id=device,
        device_id_type=pl.DeviceIdType.MESH,
    )
    copy.start()
    return copy


def signal(barrier, device):
    pl.semaphore_signal(
        barrier, inc=1, device_id=device, device_id_type=pl.DeviceIdType.MESH
    )


def rotation_rows(packed):
    low = lane_low(packed.shape)
    turned = pltpu.roll(packed, M, 1)
    a_low, b_low = jnp.where(low, packed, 0.0), jnp.where(low, turned, 0.0)
    a_high, b_high = jnp.where(low, 0.0, turned), jnp.where(low, 0.0, packed)
    rows = jnp.concatenate([a_low, b_low[:32], a_high, b_high[:32], b_low[32:], b_high[32:]], 0)
    high, rest = split(rows)
    return jnp.concatenate([high, rest], 0)


def stiff_rows(value):
    high = value.astype(BF16).astype(F32)
    blank = jnp.zeros((8, value.shape[1]), F32)
    return jnp.concatenate([high, high, value - high, blank], 0).astype(BF16)


def stiffness_band(window, stiff_ref, link_ref):
    row = lax.broadcasted_iota(jnp.int32, (LANES, LANES), 0)
    col = lax.broadcasted_iota(jnp.int32, (LANES, LANES), 1)
    far = (row - col).astype(F32)
    weight = jnp.where(row == col + 1, window[1:2], 0.0) + jnp.where(
        far == window[3:4], window[2:3], 0.0
    )
    both = weight + weight.T
    total = jnp.sum(both, 1, keepdims=True)
    stiff_ref[...] = jnp.where(row == col, window[0:1] + total, 0.0) - both
    link = jnp.sum(jnp.where(row == col, window[4:5], 0.0), 1, keepdims=True)
    link_ref[...] = jnp.broadcast_to(link, (LANES, LANES))
    lane = lax.broadcasted_iota(jnp.int32, (PAD, LANES), 1)

    def place(rows, inner, top, bottom):
        out = jnp.where(lane < HALF, pltpu.roll(rows, (LANES - inner) % LANES, 1), 0.0)
        out = jnp.where(
            (lane >= PAD) & (lane < PAD + REACH), pltpu.roll(rows, (LANES + PAD - top) % LANES, 1), out
        )
        at = PAD + REACH
        return jnp.where(
            (lane >= at) & (lane < at + REACH), pltpu.roll(rows, (LANES + at - bottom) % LANES, 1), out
        )

    near = stiff_ref[REACH : REACH + PAD, :]
    other = stiff_ref[REACH + HALF : REACH + HALF + PAD, :]
    near = place(near, REACH, 0, REACH + HALF)
    other = place(other, REACH + HALF, HALF, REACH + 2 * HALF)
    band = jnp.concatenate([near, other], 0)[:, : PAD + 2 * REACH]
    high = band.astype(BF16).astype(F32)
    terms = [high, band - high, high, jnp.zeros((2 * PAD, 8), F32)]
    links = jnp.where(
        lane < M, link_ref[REACH : REACH + PAD, :], link_ref[REACH + HALF : REACH + HALF + PAD, :]
    )
    return jnp.concatenate(terms, 1).astype(BF16), links


def step_kernel(
    x_ref,
    w_ref,
    p_ref,
    rot_ref,
    edge_ref,
    window_ref,
    four_ref,
    back_ref,
    slots_ref,
    next_ref,
    res_ref,
    ritz_ref,
    xw_ref,
    pp_ref,
    rxw_ref,
    rpp_ref,
    rall_ref,
    right_ref,
    slot_ref,
    proj_ref,
    stiff_ref,
    low_ref,
    high_ref,
    left_in_ref,
    right_in_ref,
    edge_in_ref,
    band_ref,
    link_ref,
    back_block_ref,
    back_res_ref,
    got_block_ref,
    got_res_ref,
    sums_ref,
    part_ref,
    all_ref,
    rows_ref,
    sends,
    recvs,
    locals_,
):
    spans, elems = SPANS, lax.axis_size("elem")
    me, elem = lax.axis_index("span"), lax.axis_index("elem")
    ex, ez, ec = me // 16, lax.rem(me // 2, 8), lax.rem(me, 2)
    dofs = x_ref.shape[1]
    share = 2 * HALF

    up, down = me + 1, me + spans - 1
    after = {"span": lax.rem(up, spans), "elem": lax.rem(elem + up // spans, elems)}
    before = {
        "span": lax.rem(down, spans),
        "elem": lax.rem(elem + elems - 1 + down // spans, elems),
    }

    def at(x, z, c):
        return {"span": (x * 8 + z) * 2 + c}

    def elem_at(step):
        return lax.rem(elem + step, elems)

    barrier = pltpu.get_barrier_semaphore()

    def greet(step, _):
        signal(barrier, {"span": lax.rem(me + step, spans)})
        return 0

    lax.fori_loop(1, spans, greet, 0)
    for step in range(1, elems):
        signal(barrier, {"elem": elem_at(step)})
    signal(barrier, after)
    signal(barrier, before)

    p = p_ref[...]
    moved = pltpu.roll(p, dofs - HALF, 1)
    for block in range(dofs // LANES):
        cut = slice(block * LANES, (block + 1) * LANES)
        xw_ref[cut, :] = jnp.concatenate([x_ref[:, cut], w_ref[:, cut]], 0).T
        pp_ref[cut, :] = jnp.concatenate([p[:, cut], moved[:, cut]], 0).T
    slot_ref[...] = jnp.zeros_like(slot_ref)

    pieces = [
        (xw_ref, 0, rxw_ref.at[pl.ds(0, HALF)]),
        (xw_ref, HALF, rxw_ref.at[pl.ds(HALF, HALF)]),
        (pp_ref, 0, rpp_ref),
    ]
    own = [pltpu.make_async_copy(rot_ref, rall_ref.at[ex, ez, ec], locals_.at[3])]
    for number, (src, offset, dst) in enumerate(pieces):
        own.append(
            pltpu.make_async_copy(
                src.at[pl.ds(me * share + offset, HALF)], dst.at[:, me], locals_.at[number]
            )
        )
    for copy in own:
        copy.start()
    pl.semaphore_wait(barrier, spans - 1 + elems - 1 + 2)

    for step in range(1, 8):
        where = at(ex, lax.rem(ez + step, 8), ec)
        send(rot_ref, rall_ref.at[ex, ez, ec], sends.at[3], recvs.at[3], where)
    edge = send(edge_ref, edge_in_ref, sends.at[6], recvs.at[6], {"elem": elem_at(1)})

    def scatter(number):
        src, offset, dst = pieces[number]

        def body(step, _):
            other = lax.rem(me + step, spans)
            send(
                src.at[pl.ds(other * share + offset, HALF)],
                dst.at[:, me],
                sends.at[number],
                recvs.at[number],
                {"span": other},
            )
            return 0

        lax.fori_loop(1, spans, body, 0)

    rest_z, rest_x = rall_ref.at[0, pl.ds(0, 7), 0], rall_ref.at[pl.ds(0, 3), :, 0]
    scatter(0)
    own[0].wait()
    arrived(rest_z, recvs.at[3])
    for step in range(1, 4):
        mine = rall_ref.at[ex, :, ec]
        send(mine, mine, sends.at[4], recvs.at[4], at(lax.rem(ex + step, 4), ez, ec))
    scatter(1)
    scatter(2)
    edge.wait()
    lane8 = lax.broadcasted_iota(jnp.int32, (8, LANES), 1)
    window = jnp.where((lane8 < REACH) & (me == 0), edge_in_ref[...], window_ref[...])
    band, links = stiffness_band(window, band_ref, link_ref)
    arrived(rest_x, recvs.at[4])
    mine = rall_ref.at[:, :, ec]
    cross = send(mine, mine, sends.at[5], recvs.at[5], at(ex, ez, 1 - ec))

    def prepare(core):
        def body(step, _):
            rows = rotation_rows(rall_ref[step // 8, lax.rem(step, 8), core])
            right_ref[2 * step + core] = rows
            return 0

        lax.fori_loop(0, spans // 2, body, 0)

    prepare(ec)

    def transform(number):
        _, _, dst = pieces[number]
        own[1 + number].wait()
        arrived(dst.at[:, pl.ds(0, spans - 1)], recvs.at[number])
        group = 4

        def body(step, _):
            rows = jnp.concatenate([dst[step * group + q] for q in range(group)], 1)
            out = jnp.dot(four_ref[...], right_rows(rows), preferred_element_type=F32)
            for q in range(group):
                slot_ref[number, pl.ds(step * group + q, spans, stride=PAD), :] = out[
                    :, q * LANES : (q + 1) * LANES
                ]
            return 0

        lax.fori_loop(0, HALF // group, body, 0)

    transform(0)
    cross.wait()
    prepare(1 - ec)
    transform(1)
    transform(2)

    def rotate(j, _):
        cut = pl.ds(pl.multiple_of(j * PAD, 8), PAD)
        rows = jnp.concatenate([slot_ref[number, cut, :] for number in range(3)], 1)
        high = rows.astype(BF16).astype(F32)
        left = jnp.concatenate([high, rows - high], 0).astype(BF16)
        out = jnp.dot(
            jnp.concatenate([left, left], 1), right_ref[j], preferred_element_type=F32
        )
        out = out[:PAD] + out[PAD:]
        proj_ref[cut, :] = out
        low_ref[j] = out[:REACH]
        high_ref[j] = out[HALF - REACH : HALF]
        return 0

    lax.fori_loop(0, spans, rotate, 0, unroll=2)
    halo = [
        send(high_ref, left_in_ref, sends.at[7], recvs.at[7], after),
        send(low_ref, right_in_ref, sends.at[8], recvs.at[8], before),
    ]

    def inverse(source, target):
        group = 4

        def body(step, _):
            rows = [source(pl.ds(step * group + q, spans, stride=PAD)) for q in range(group)]
            out = jnp.dot(
                back_ref[...], right_rows(jnp.concatenate(rows, 1)), preferred_element_type=F32
            )
            for q in range(group):
                target[step * group + q] = out[:, q * LANES : (q + 1) * LANES]
            return 0

        lax.fori_loop(0, HALF // group, body, 0)

    def give_back(source, target, number):
        copy = pltpu.make_async_copy(source.at[:, me], target.at[me], locals_.at[number])
        copy.start()

        def body(step, _):
            other = lax.rem(me + step, spans)
            send(
                source.at[:, other],
                target.at[me],
                sends.at[number],
                recvs.at[number],
                {"span": other},
            )
            return 0

        lax.fori_loop(1, spans, body, 0)
        return copy

    inverse(lambda rows: proj_ref[rows, :], back_block_ref)
    own_block = give_back(back_block_ref, got_block_ref, 9)

    for copy in halo:
        copy.wait()
    half = lane_low((REACH, LANES))
    low = lane_low((PAD, LANES))
    kept = lax.broadcasted_iota(jnp.int32, (PAD, LANES), 0) < HALF
    side = lane_low((1, LANES))

    def stiffen(step, _):
        group = 4
        parts = []
        for q in range(group):
            j = step * group + q
            rows = proj_ref[pl.ds(pl.multiple_of(j * PAD, 8), PAD), :]
            top = pltpu.roll(jnp.where(half, high_ref[j], left_in_ref[j]), M, 1)
            bottom = pltpu.roll(jnp.where(half, right_in_ref[j], low_ref[j]), M, 1)
            parts.append(jnp.concatenate([rows, top, bottom], 0))
        out = jnp.dot(
            band, stiff_rows(jnp.concatenate(parts, 1)), preferred_element_type=F32
        )
        for q in range(group):
            j = step * group + q
            cut = slice(q * LANES, (q + 1) * LANES)
            rows = parts[q][:PAD]
            stiff = jnp.where(low, out[:PAD, cut], out[PAD:, cut])
            stiff = stiff + slots_ref[pl.ds(j, 1), :] * links * rows
            stiff_ref[pl.ds(pl.multiple_of(j * PAD, 8), PAD), :] = stiff
            energy = jnp.sum(jnp.where(kept, rows * stiff, 0.0), 0, keepdims=True)
            weight = jnp.sum(jnp.where(kept, rows * rows, 0.0), 0, keepdims=True)
            energy = energy + pltpu.roll(energy, M, 1)
            weight = weight + pltpu.roll(weight, M, 1)
            sums_ref[pl.ds(j, 1), :] = jnp.where(side, energy, weight)
        return 0

    lax.fori_loop(0, spans // 4, stiffen, 0)

    rest = pl.ds(0, 7)
    part_ref[0, elem] = sums_ref[pl.ds(pl.multiple_of(elem * 8, 8), 8), :]
    for step in range(1, elems):
        other = elem_at(step)
        send(
            sums_ref.at[pl.ds(other * 8, 8)],
            part_ref.at[0, elem],
            sends.at[10],
            recvs.at[10],
            {"elem": other},
        )
    arrived(part_ref.at[0, rest], recvs.at[10])
    part_ref[1, ez] = jnp.sum(part_ref[0], 0)
    for step in range(1, 8):
        where = at(ex, lax.rem(ez + step, 8), ec)
        send(part_ref.at[1, ez], part_ref.at[1, ez], sends.at[11], recvs.at[11], where)
    arrived(part_ref.at[1, rest], recvs.at[11])
    pair = ex * 2 + ec
    part_ref[2, pair] = jnp.sum(part_ref[1], 0)
    for step in range(1, 8):
        other = lax.rem(pair + step, 8)
        where = at(other // 2, ez, lax.rem(other, 2))
        send(part_ref.at[2, pair], part_ref.at[2, pair], sends.at[12], recvs.at[12], where)
    arrived(part_ref.at[2, rest], recvs.at[12])
    total = jnp.sum(part_ref[2], 0)
    ritz = total / (pltpu.roll(total, M, 1) + 1e-06)
    ritz = jnp.where(lane_low((8, LANES)), ritz, pltpu.roll(ritz, M, 1))
    all_ref[elem] = ritz
    for step in range(1, elems):
        send(
            all_ref.at[elem], all_ref.at[elem], sends.at[13], recvs.at[13], {"elem": elem_at(step)}
        )
    arrived(all_ref.at[rest], recvs.at[13])
    ritz = jnp.concatenate([all_ref[g] for g in range(8)], 0)
    sums = lax.broadcasted_iota(jnp.int32, ritz.shape, 0) == me
    ritz_ref[...] = jnp.sum(jnp.where(sums, ritz, 0.0), 0, keepdims=True)

    inverse(lambda rows: stiff_ref[rows, :] - ritz * proj_ref[rows, :], back_res_ref)
    own_res = give_back(back_res_ref, got_res_ref, 14)

    def unpack(source, target):
        def body(i, _):
            rows = source[i]
            both = jnp.concatenate([rows, pltpu.roll(rows, M, 1)], 0)
            rows_ref[pl.ds(pl.multiple_of(i * share, 8), share), :] = both
            return 0

        lax.fori_loop(0, spans, body, 0, unroll=4)
        for block in range(dofs // LANES):
            cut = slice(block * LANES, (block + 1) * LANES)
            target[:, cut] = rows_ref[cut, :].T[:M]

    rest = pl.ds(0, spans - 1)
    own_block.wait()
    arrived(got_block_ref.at[rest], recvs.at[9])
    unpack(got_block_ref, next_ref)
    own_res.wait()
    arrived(got_res_ref.at[rest], recvs.at[14])
    unpack(got_res_ref, res_ref)

    for number, (_, _, dst) in enumerate(pieces):
        arrived(dst.at[:, rest], sends.at[number])
    arrived(rest_z, sends.at[3])
    arrived(rest_x, sends.at[4])
    arrived(got_block_ref.at[rest], sends.at[9])
    for stage in range(3):
        arrived(part_ref.at[stage, pl.ds(0, 7)], sends.at[10 + stage])
    arrived(all_ref.at[pl.ds(0, 7)], sends.at[13])
    arrived(got_res_ref.at[rest], sends.at[14])


def shape(*dims):
    return jax.ShapeDtypeStruct(dims, F32)


def on_device(
    current_block,
    search_block,
    previous_block,
    ground_spring,
    wire_tension,
    dropper_stiff,
    dropper_offset,
    span_link,
    ritz_rotation,
):
    dofs = current_block.shape[2]
    spans, elems = lax.axis_size("span"), lax.axis_size("elem")
    me, elem = lax.axis_index("span"), lax.axis_index("elem")
    share = dofs // spans
    matrix, links = fourier_np(spans)

    position = elem * dofs + jnp.arange(dofs)
    total = dofs * elems
    tension = jnp.where(position < total - 1, wire_tension, 0.0)
    dropper = jnp.where(position + dropper_offset < total, dropper_stiff, 0.0)
    coefs = jnp.stack([ground_spring, tension, dropper, dropper_offset.astype(F32), span_link])
    coefs = jnp.pad(coefs, ((0, 3), (REACH, LANES)))
    edge = coefs[:, dofs : dofs + LANES]
    window = lax.dynamic_slice(coefs, (0, me * share), (8, LANES))
    rotation = jnp.concatenate([ritz_rotation[0, :96], ritz_rotation[0, 96:]], 1)
    rows = spans * PAD
    slots = jnp.asarray(np.repeat(links[:, None], LANES, 1).astype(np.float32))

    next_block, next_residual, ritz = pl.pallas_call(
        step_kernel,
        out_shape=(shape(M, dofs), shape(M, dofs), shape(1, LANES)),
        in_specs=full(9),
        out_specs=tuple(full(3)),
        scratch_shapes=[
            VMEM((dofs, LANES), F32),
            VMEM((dofs, LANES), F32),
            VMEM((share, spans, LANES), F32),
            VMEM((HALF, spans, LANES), F32),
            VMEM((4, 8, 2, 96, LANES), F32),
            VMEM((spans, 768, LANES), BF16),
            VMEM((3, rows, LANES), F32),
            VMEM((rows, LANES), F32),
            VMEM((rows, LANES), F32),
            VMEM((spans, REACH, LANES), F32),
            VMEM((spans, REACH, LANES), F32),
            VMEM((spans, REACH, LANES), F32),
            VMEM((spans, REACH, LANES), F32),
            VMEM((8, LANES), F32),
            VMEM((LANES, LANES), F32),
            VMEM((LANES, LANES), F32),
            VMEM((HALF, spans, LANES), F32),
            VMEM((HALF, spans, LANES), F32),
            VMEM((spans, HALF, LANES), F32),
            VMEM((spans, HALF, LANES), F32),
            VMEM((spans, LANES), F32),
            VMEM((3, 8, 8, LANES), F32),
            VMEM((8, 8, LANES), F32),
            VMEM((dofs, LANES), F32),
            pltpu.SemaphoreType.DMA((15,)),
            pltpu.SemaphoreType.DMA((15,)),
            pltpu.SemaphoreType.DMA((15,)),
        ],
        compiler_params=params(0),
    )(
        current_block[0],
        search_block[0],
        previous_block[0],
        rotation,
        edge,
        window,
        jnp.asarray(left_terms(matrix)),
        jnp.asarray(left_terms(matrix.T)),
        slots,
    )
    return (next_block[None], next_residual[None], ritz[:, :M])


def solution(mesh):
    return jax.shard_map(
        on_device,
        mesh=mesh,
        in_specs=(
            P("span", None, "elem"),
            P("span", None, "elem"),
            P("span", None, "elem"),
            P("elem"),
            P("elem"),
            P("elem"),
            P("elem"),
            P("elem"),
            P("span", None, None),
        ),
        out_specs=(P("span", None, "elem"), P("span", None, "elem"), P("span", None)),
        check_vma=False,
    )
```

```python
import functools
import math

import jax
import jax.numpy as jnp
import ml_dtypes
import numpy as np
from jax import lax
from jax.experimental import pallas as pl
from jax.experimental.pallas import tpu as pltpu
from jax.sharding import PartitionSpec as P

REACH = 8
SPANS = 64
M = 64
HALF = 20
PAD = 24
LANES = 128
F32 = jnp.float32
BF16 = jnp.bfloat16
VMEM = pltpu.VMEM


def split_np(matrix):
    high = matrix.astype(np.float32).astype(ml_dtypes.bfloat16)
    low = (matrix - high.astype(np.float64)).astype(ml_dtypes.bfloat16)
    return high, low


def fourier_np(count):
    half = count // 2
    row = np.arange(count)[:, None]
    col = np.arange(count)[None, :]
    wave = np.where(row <= half, row, row - half)
    phase = (wave * col % count) * (2.0 * math.pi / count)
    scaled = np.where(row <= half, np.cos(phase), np.sin(phase)) * math.sqrt(2.0 / count)
    edge = (row == 0) | (row == half)
    matrix = np.where(edge, np.cos(phase) * math.sqrt(1.0 / count), scaled)
    slots = np.arange(count)
    slot_wave = np.where(slots <= half, slots, slots - half)
    links = 2.0 * (1.0 - np.cos(slot_wave * (2.0 * math.pi / count)))
    return matrix, links


def left_terms(matrix):
    high, low = split_np(matrix)
    return np.concatenate([high, low, high], 1)


def split(value):
    high = value.astype(BF16)
    low = (value - high.astype(F32)).astype(BF16)
    return high, low


def right_rows(value):
    high, low = split(value)
    return jnp.concatenate([high, high, low], 0)


def lane_low(shape):
    return lax.broadcasted_iota(jnp.int32, shape, len(shape) - 1) < M


def full(count):
    return [pl.BlockSpec(memory_space=VMEM)] * count


def params(collective=None, limit=56):
    return pltpu.CompilerParams(
        vmem_limit_bytes=limit << 20,
        collective_id=collective,
        has_side_effects=collective is not None,
    )


def arrived(ref, sem):
    pltpu.make_async_copy(ref, ref, sem).wait()


def send(src, dst, send_sem, recv_sem, device):
    copy = pltpu.make_async_remote_copy(
        src_ref=src,
        dst_ref=dst,
        send_sem=send_sem,
        recv_sem=recv_sem,
        device_id=device,
        device_id_type=pl.DeviceIdType.MESH,
    )
    copy.start()
    return copy


def signal(barrier, device):
    pl.semaphore_signal(
        barrier, inc=1, device_id=device, device_id_type=pl.DeviceIdType.MESH
    )


def rotation_rows(packed):
    low = lane_low(packed.shape)
    turned = pltpu.roll(packed, M, 1)
    a_low, b_low = jnp.where(low, packed, 0.0), jnp.where(low, turned, 0.0)
    a_high, b_high = jnp.where(low, 0.0, turned), jnp.where(low, 0.0, packed)
    rows = jnp.concatenate([a_low, b_low[:32], a_high, b_high[:32], b_low[32:], b_high[32:]], 0)
    high, rest = split(rows)
    return jnp.concatenate([high, rest], 0)


def stiff_rows(value):
    high = value.astype(BF16).astype(F32)
    blank = jnp.zeros((8, value.shape[1]), F32)
    return jnp.concatenate([high, high, value - high, blank], 0).astype(BF16)


def stiffness_band(window, stiff_ref, link_ref):
    row = lax.broadcasted_iota(jnp.int32, (LANES, LANES), 0)
    col = lax.broadcasted_iota(jnp.int32, (LANES, LANES), 1)
    far = (row - col).astype(F32)
    weight = jnp.where(row == col + 1, window[1], 0.0) + jnp.where(
        far == window[3], window[2], 0.0
    )
    both = weight + weight.T
    total = jnp.sum(both, 1, keepdims=True)
    stiff_ref[...] = jnp.where(row == col, window[0] + total, 0.0) - both
    link = jnp.sum(jnp.where(row == col, window[4], 0.0), 1, keepdims=True)
    link_ref[...] = jnp.broadcast_to(link, (LANES, LANES))
    lane = lax.broadcasted_iota(jnp.int32, (PAD, LANES), 1)

    def place(rows, inner, top, bottom):
        out = jnp.where(lane < HALF, pltpu.roll(rows, (LANES - inner) % LANES, 1), 0.0)
        out = jnp.where(
            (lane >= PAD) & (lane < PAD + REACH), pltpu.roll(rows, (LANES + PAD - top) % LANES, 1), out
        )
        at = PAD + REACH
        return jnp.where(
            (lane >= at) & (lane < at + REACH), pltpu.roll(rows, (LANES + at - bottom) % LANES, 1), out
        )

    near = stiff_ref[REACH : REACH + PAD, :]
    other = stiff_ref[REACH + HALF : REACH + HALF + PAD, :]
    near = place(near, REACH, 0, REACH + HALF)
    other = place(other, REACH + HALF, HALF, REACH + 2 * HALF)
    band = jnp.concatenate([near, other], 0)[:, : PAD + 2 * REACH]
    high = band.astype(BF16).astype(F32)
    terms = [high, band - high, high, jnp.zeros((2 * PAD, 8), F32)]
    links = jnp.where(
        lane < M, link_ref[REACH : REACH + PAD, :], link_ref[REACH + HALF : REACH + HALF + PAD, :]
    )
    return jnp.concatenate(terms, 1).astype(BF16), links


def unpack(source, rows_ref, target):
    share = 2 * HALF

    def body(i, _):
        rows = source[i]
        both = jnp.concatenate([rows, pltpu.roll(rows, M, 1)], 0)
        rows_ref[pl.ds(pl.multiple_of(i * share, 8), share), :] = both
        return 0

    lax.fori_loop(0, SPANS, body, 0, unroll=8)
    for block in range(rows_ref.shape[0] // LANES):
        cut = slice(block * LANES, (block + 1) * LANES)
        target[:, cut] = rows_ref[cut, :].T[:M]


def finish_kernel(block_ref, got_ref, next_ref, res_ref, rows_ref):
    next_ref[...] = block_ref[...]
    unpack(got_ref, rows_ref, res_ref)


def step_kernel(
    x_ref,
    w_ref,
    p_ref,
    coefs_refs,
    offset_ref,
    turned_ref,
    four_ref,
    back_ref,
    slots_ref,
    next_ref,
    got_res_ref,
    ritz_ref,
    pack_ref,
    got_ref,
    coef_ref,
    edge_ref,
    rot_ref,
    rall_ref,
    right_ref,
    slot_ref,
    proj_ref,
    stiff_ref,
    low_ref,
    high_ref,
    left_in_ref,
    right_in_ref,
    edge_in_ref,
    band_ref,
    link_ref,
    back_block_ref,
    back_res_ref,
    got_block_ref,
    sums_ref,
    part_ref,
    all_ref,
    rows_ref,
    sends,
    recvs,
    locals_,
):
    spans, elems = SPANS, lax.axis_size("elem")
    me, elem = lax.axis_index("span"), lax.axis_index("elem")
    ex, ez, ec = me // 16, lax.rem(me // 2, 8), lax.rem(me, 2)
    dofs = x_ref.shape[1]
    share = 2 * HALF

    up, down = me + 1, me + spans - 1
    after = {"span": lax.rem(up, spans), "elem": lax.rem(elem + up // spans, elems)}
    before = {
        "span": lax.rem(down, spans),
        "elem": lax.rem(elem + elems - 1 + down // spans, elems),
    }

    def at(x, z, c):
        return {"span": (x * 8 + z) * 2 + c}

    def elem_at(step):
        return lax.rem(elem + step, elems)

    barrier = pltpu.get_barrier_semaphore()

    def greet(step, _):
        signal(barrier, {"span": lax.rem(me + step, spans)})
        return 0

    lax.fori_loop(1, spans, greet, 0)
    for step in range(1, elems):
        signal(barrier, {"elem": elem_at(step)})
    signal(barrier, after)
    signal(barrier, before)

    rot_ref[...] = jnp.concatenate([turned_ref[:, :96], turned_ref[:, 96:]], 0).T
    own_rot = pltpu.make_async_copy(rot_ref, rall_ref.at[ex, ez, ec], locals_.at[3])
    own_rot.start()
    pl.semaphore_wait(barrier, spans - 1 + elems - 1 + 2)
    for step in range(1, 8):
        where = at(ex, lax.rem(ez + step, 8), ec)
        send(rot_ref, rall_ref.at[ex, ez, ec], sends.at[3], recvs.at[3], where)

    count = dofs // LANES
    for block in range(count):
        cut = slice(block * LANES, (block + 1) * LANES)
        pack_ref[cut, :] = jnp.concatenate([x_ref[:, cut], w_ref[:, cut]], 0).T

    def packed_at(device, number):
        row = device * share + (number % 2) * HALF + (number // 2) * dofs
        return pack_ref.at[pl.ds(row, HALF)]

    def message(q):
        number, step = q // (spans - 1), lax.rem(q, spans - 1) + 1
        other = lax.rem(me + step, spans)
        send(
            packed_at(other, number),
            got_ref.at[pl.ds(number * HALF, HALF), me],
            sends.at[number],
            recvs.at[number],
            {"span": other},
        )

    def messages(first, last):
        def body(q, _):
            message(q)
            return 0

        lax.fori_loop(first, last, body, 0)

    rest_z, rest_x = rall_ref.at[0, pl.ds(0, 7), 0], rall_ref.at[pl.ds(0, 3), :, 0]
    rest_c = rall_ref.at[:, :, 0]
    messages(0, spans - 1)
    own_rot.wait()
    arrived(rest_z, recvs.at[3])
    for step in range(1, 4):
        mine = rall_ref.at[ex, :, ec]
        send(mine, mine, sends.at[4], recvs.at[4], at(lax.rem(ex + step, 4), ez, ec))
    messages(spans - 1, 2 * (spans - 1))
    p = p_ref[...]
    moved = pltpu.roll(p, dofs - HALF, 1)
    for block in range(count):
        cut = slice(block * LANES, (block + 1) * LANES)
        below = slice(dofs + block * LANES, dofs + (block + 1) * LANES)
        pack_ref[below, :] = jnp.concatenate([p[:, cut], moved[:, cut]], 0).T
    messages(2 * (spans - 1), 3 * (spans - 1))
    own = []
    for number in range(3):
        target = got_ref.at[pl.ds(number * HALF, HALF), me]
        own.append(pltpu.make_async_copy(packed_at(me, number), target, locals_.at[number]))
        own[number].start()

    ground_ref, tension_ref, dropper_ref, link_in_ref = coefs_refs
    grid = (count, LANES)
    position = elem * dofs + LANES * lax.broadcasted_iota(jnp.int32, grid, 0)
    position = position + lax.broadcasted_iota(jnp.int32, grid, 1)
    offset = offset_ref[...]
    values = [
        ground_ref[...],
        jnp.where(position < dofs * elems - 1, tension_ref[...], 0.0),
        jnp.where(position + offset < dofs * elems, dropper_ref[...], 0.0),
        offset.astype(F32),
        link_in_ref[...],
    ]
    coef_ref[...] = jnp.zeros_like(coef_ref)
    edge_ref[...] = jnp.zeros_like(edge_ref)
    for number, value in enumerate(values):
        coef_ref[number, 1 : 1 + count, :] = value
        edge_ref[number : number + 1, :] = value[count - 1 :]
    edge = send(edge_ref, edge_in_ref, sends.at[6], recvs.at[6], {"elem": elem_at(1)})

    slot_ref[...] = jnp.zeros_like(slot_ref)

    edge.wait()
    for number in range(5):
        coef_ref[number, 0:1, :] = edge_in_ref[number : number + 1, :]
    start = LANES - REACH + me * share
    row, kept_lanes = start // LANES, LANES - lax.rem(start, LANES)
    turn = lax.rem(kept_lanes, LANES)
    lane = lax.broadcasted_iota(jnp.int32, (1, LANES), 1)
    window = []
    for number in range(5):
        one = pltpu.roll(coef_ref[number, pl.ds(row, 1), :], turn, 1)
        two = pltpu.roll(coef_ref[number, pl.ds(row + 1, 1), :], turn, 1)
        window.append(jnp.where(lane < kept_lanes, one, two))
    band, links = stiffness_band(window, band_ref, link_ref)
    arrived(rest_x, recvs.at[4])
    mine = rall_ref.at[:, :, ec]
    cross = send(mine, mine, sends.at[5], recvs.at[5], at(ex, ez, 1 - ec))

    def prepare(core):
        def body(step, _):
            rows = rotation_rows(rall_ref[step // 8, lax.rem(step, 8), core])
            right_ref[2 * step + core] = rows
            return 0

        lax.fori_loop(0, spans // 2, body, 0, unroll=4)

    prepare(ec)

    def transform(number):
        own[number].wait()
        arrived(got_ref.at[pl.ds(0, HALF), pl.ds(0, spans - 1)], recvs.at[number])
        group = 4

        def body(step, _):
            rows = jnp.concatenate(
                [got_ref[number * HALF + step * group + q] for q in range(group)], 1
            )
            out = jnp.dot(four_ref[...], right_rows(rows), preferred_element_type=F32)
            for q in range(group):
                slot_ref[number, pl.ds(step * group + q, spans, stride=PAD), :] = out[
                    :, q * LANES : (q + 1) * LANES
                ]
            return 0

        lax.fori_loop(0, HALF // group, body, 0, unroll=5)

    transform(0)
    transform(1)
    transform(2)

    def rotate(step, _, core):
        j = 2 * step + core
        cut = pl.ds(pl.multiple_of(j * PAD, 8), PAD)
        rows = jnp.concatenate([slot_ref[number, cut, :] for number in range(3)], 1)
        high = rows.astype(BF16).astype(F32)
        left = jnp.concatenate([high, rows - high], 0).astype(BF16)
        out = jnp.dot(
            jnp.concatenate([left, left], 1), right_ref[j], preferred_element_type=F32
        )
        out = out[:PAD] + out[PAD:]
        proj_ref[cut, :] = out
        low_ref[j] = out[:REACH]
        high_ref[j] = out[HALF - REACH : HALF]
        return 0

    lax.fori_loop(0, spans // 2, functools.partial(rotate, core=ec), 0, unroll=4)
    cross.wait_recv()
    prepare(1 - ec)
    lax.fori_loop(0, spans // 2, functools.partial(rotate, core=1 - ec), 0, unroll=4)
    halo = [
        send(high_ref, left_in_ref, sends.at[7], recvs.at[7], after),
        send(low_ref, right_in_ref, sends.at[8], recvs.at[8], before),
    ]

    def inverse(source, target):
        group = 4

        def body(step, _):
            rows = [source(pl.ds(step * group + q, spans, stride=PAD)) for q in range(group)]
            out = jnp.dot(
                back_ref[...], right_rows(jnp.concatenate(rows, 1)), preferred_element_type=F32
            )
            for q in range(group):
                target[step * group + q] = out[:, q * LANES : (q + 1) * LANES]
            return 0

        lax.fori_loop(0, HALF // group, body, 0, unroll=5)

    def give_back(source, target, number, first, last):
        def body(step, _):
            other = lax.rem(me + step, spans)
            send(
                source.at[:, other],
                target.at[me],
                sends.at[number],
                recvs.at[number],
                {"span": other},
            )
            return 0

        lax.fori_loop(first, last, body, 0)

    def give_block(first, last):
        give_back(back_block_ref, got_block_ref, 9, first, last)

    inverse(lambda rows: proj_ref[rows, :], back_block_ref)
    own_block = pltpu.make_async_copy(
        back_block_ref.at[:, me], got_block_ref.at[me], locals_.at[9]
    )
    own_block.start()
    give_block(1, 25)

    for copy in halo:
        copy.wait()
    half = lane_low((REACH, LANES))
    low = lane_low((PAD, LANES))
    kept = lax.broadcasted_iota(jnp.int32, (PAD, LANES), 0) < HALF
    side = lane_low((1, LANES))

    def stiffen(step, _):
        group = 4
        parts = []
        for q in range(group):
            j = step * group + q
            rows = proj_ref[pl.ds(pl.multiple_of(j * PAD, 8), PAD), :]
            top = pltpu.roll(jnp.where(half, high_ref[j], left_in_ref[j]), M, 1)
            bottom = pltpu.roll(jnp.where(half, right_in_ref[j], low_ref[j]), M, 1)
            parts.append(jnp.concatenate([rows, top, bottom], 0))
        out = jnp.dot(
            band, stiff_rows(jnp.concatenate(parts, 1)), preferred_element_type=F32
        )
        for q in range(group):
            j = step * group + q
            cut = slice(q * LANES, (q + 1) * LANES)
            rows = parts[q][:PAD]
            stiff = jnp.where(low, out[:PAD, cut], out[PAD:, cut])
            stiff = stiff + slots_ref[pl.ds(j, 1), :] * links * rows
            stiff_ref[pl.ds(pl.multiple_of(j * PAD, 8), PAD), :] = stiff
            energy = jnp.sum(jnp.where(kept, rows * stiff, 0.0), 0, keepdims=True)
            weight = jnp.sum(jnp.where(kept, rows * rows, 0.0), 0, keepdims=True)
            energy = energy + pltpu.roll(energy, M, 1)
            weight = weight + pltpu.roll(weight, M, 1)
            sums_ref[pl.ds(j, 1), :] = jnp.where(side, energy, weight)
        return 0

    lax.fori_loop(0, spans // 4, stiffen, 0, unroll=4)

    rest = pl.ds(0, 7)
    part_ref[0, elem] = sums_ref[pl.ds(pl.multiple_of(elem * 8, 8), 8), :]
    for step in range(1, elems):
        other = elem_at(step)
        send(
            sums_ref.at[pl.ds(other * 8, 8)],
            part_ref.at[0, elem],
            sends.at[10],
            recvs.at[10],
            {"elem": other},
        )
    give_block(25, 38)
    arrived(part_ref.at[0, rest], recvs.at[10])
    part_ref[1, ez] = jnp.sum(part_ref[0], 0)
    for step in range(1, 8):
        where = at(ex, lax.rem(ez + step, 8), ec)
        send(part_ref.at[1, ez], part_ref.at[1, ez], sends.at[11], recvs.at[11], where)
    give_block(38, 51)
    arrived(part_ref.at[1, rest], recvs.at[11])
    pair = ex * 2 + ec
    part_ref[2, pair] = jnp.sum(part_ref[1], 0)
    for step in range(1, 8):
        other = lax.rem(pair + step, 8)
        where = at(other // 2, ez, lax.rem(other, 2))
        send(part_ref.at[2, pair], part_ref.at[2, pair], sends.at[12], recvs.at[12], where)
    give_block(51, 64)
    arrived(part_ref.at[2, rest], recvs.at[12])
    total = jnp.sum(part_ref[2], 0)
    ritz = total / (pltpu.roll(total, M, 1) + 1e-06)
    ritz = jnp.where(lane_low((8, LANES)), ritz, pltpu.roll(ritz, M, 1))
    all_ref[elem] = ritz
    for step in range(1, elems):
        send(
            all_ref.at[elem], all_ref.at[elem], sends.at[13], recvs.at[13], {"elem": elem_at(step)}
        )
    arrived(all_ref.at[rest], recvs.at[13])
    ritz = jnp.concatenate([all_ref[g] for g in range(8)], 0)
    sums = lax.broadcasted_iota(jnp.int32, ritz.shape, 0) == me
    ritz_ref[...] = jnp.sum(jnp.where(sums, ritz, 0.0), 0, keepdims=True)

    inverse(lambda rows: stiff_ref[rows, :] - ritz * proj_ref[rows, :], back_res_ref)
    own_res = pltpu.make_async_copy(back_res_ref.at[:, me], got_res_ref.at[me], locals_.at[14])
    own_res.start()
    give_back(back_res_ref, got_res_ref, 14, 1, spans)

    rest = pl.ds(0, spans - 1)
    own_block.wait()
    arrived(got_block_ref.at[rest], recvs.at[9])
    unpack(got_block_ref, rows_ref, next_ref)
    own_res.wait()
    arrived(got_res_ref.at[rest], recvs.at[14])

    for number in range(3):
        arrived(got_ref.at[pl.ds(0, HALF), rest], sends.at[number])
    arrived(rest_z, sends.at[3])
    arrived(rest_x, sends.at[4])
    arrived(rest_c, sends.at[5])
    arrived(got_block_ref.at[rest], sends.at[9])
    for stage in range(3):
        arrived(part_ref.at[stage, pl.ds(0, 7)], sends.at[10 + stage])
    arrived(all_ref.at[pl.ds(0, 7)], sends.at[13])
    arrived(got_res_ref.at[rest], sends.at[14])


def shape(*dims):
    return jax.ShapeDtypeStruct(dims, F32)


def on_device(
    current_block,
    search_block,
    previous_block,
    ground_spring,
    wire_tension,
    dropper_stiff,
    dropper_offset,
    span_link,
    ritz_rotation,
):
    dofs = current_block.shape[2]
    spans = lax.axis_size("span")
    share = dofs // spans
    matrix, links = fourier_np(spans)

    grid = (dofs // LANES, LANES)
    rows = spans * PAD
    slots = jnp.asarray(np.repeat(links[:, None], LANES, 1).astype(np.float32))

    block, got, ritz = pl.pallas_call(
        step_kernel,
        out_shape=(shape(M, dofs), shape(spans, HALF, LANES), shape(1, LANES)),
        in_specs=full(3) + [full(4)] + full(5),
        out_specs=tuple(full(3)),
        scratch_shapes=[
            VMEM((2 * dofs, LANES), F32),
            VMEM((3 * HALF, spans, LANES), F32),
            VMEM((5, 24, LANES), F32),
            VMEM((8, LANES), F32),
            VMEM((96, LANES), F32),
            VMEM((4, 8, 2, 96, LANES), F32),
            VMEM((spans, 768, LANES), BF16),
            VMEM((3, rows, LANES), F32),
            VMEM((rows, LANES), F32),
            VMEM((rows, LANES), F32),
            VMEM((spans, REACH, LANES), F32),
            VMEM((spans, REACH, LANES), F32),
            VMEM((spans, REACH, LANES), F32),
            VMEM((spans, REACH, LANES), F32),
            VMEM((8, LANES), F32),
            VMEM((LANES, LANES), F32),
            VMEM((LANES, LANES), F32),
            VMEM((HALF, spans, LANES), F32),
            VMEM((HALF, spans, LANES), F32),
            VMEM((spans, HALF, LANES), F32),
            VMEM((spans, LANES), F32),
            VMEM((3, 8, 8, LANES), F32),
            VMEM((8, 8, LANES), F32),
            VMEM((dofs, LANES), F32),
            pltpu.SemaphoreType.DMA((15,)),
            pltpu.SemaphoreType.DMA((15,)),
            pltpu.SemaphoreType.DMA((15,)),
        ],
        compiler_params=params(0),
    )(
        current_block[0],
        search_block[0],
        previous_block[0],
        [
            coef.reshape(grid)
            for coef in (ground_spring, wire_tension, dropper_stiff, span_link)
        ],
        dropper_offset.reshape(grid),
        ritz_rotation[0].T,
        jnp.asarray(left_terms(matrix)),
        jnp.asarray(left_terms(matrix.T)),
        slots,
    )
    next_block, next_residual = pl.pallas_call(
        finish_kernel,
        out_shape=(shape(M, dofs), shape(M, dofs)),
        in_specs=full(2),
        out_specs=tuple(full(2)),
        scratch_shapes=[VMEM((dofs, LANES), F32)],
        compiler_params=params(limit=16),
    )(block, got)
    return (next_block[None], next_residual[None], ritz[:, :M])


def solution(mesh):
    return jax.shard_map(
        on_device,
        mesh=mesh,
        in_specs=(
            P("span", None, "elem"),
            P("span", None, "elem"),
            P("span", None, "elem"),
            P("elem"),
            P("elem"),
            P("elem"),
            P("elem"),
            P("elem"),
            P("span", None, None),
        ),
        out_specs=(P("span", None, "elem"), P("span", None, "elem"), P("span", None)),
        check_vma=False,
    )
```

```python
import functools
import math

import jax
import jax.numpy as jnp
import ml_dtypes
import numpy as np
from jax import lax
from jax.experimental import pallas as pl
from jax.experimental.pallas import tpu as pltpu
from jax.sharding import PartitionSpec as P

REACH = 8
SPANS = 64
M = 64
HALF = 20
PAD = 24
LANES = 128
F32 = jnp.float32
BF16 = jnp.bfloat16
VMEM = pltpu.VMEM


def split_np(matrix):
    high = matrix.astype(np.float32).astype(ml_dtypes.bfloat16)
    low = (matrix - high.astype(np.float64)).astype(ml_dtypes.bfloat16)
    return high, low


def fourier_np(count):
    half = count // 2
    row = np.arange(count)[:, None]
    col = np.arange(count)[None, :]
    wave = np.where(row <= half, row, row - half)
    phase = (wave * col % count) * (2.0 * math.pi / count)
    scaled = np.where(row <= half, np.cos(phase), np.sin(phase)) * math.sqrt(2.0 / count)
    edge = (row == 0) | (row == half)
    matrix = np.where(edge, np.cos(phase) * math.sqrt(1.0 / count), scaled)
    slots = np.arange(count)
    slot_wave = np.where(slots <= half, slots, slots - half)
    links = 2.0 * (1.0 - np.cos(slot_wave * (2.0 * math.pi / count)))
    return matrix, links


def left_terms(matrix):
    high, low = split_np(matrix)
    return np.concatenate([high, low, high], 1)


def split(value):
    high = value.astype(BF16)
    low = (value - high.astype(F32)).astype(BF16)
    return high, low


def right_rows(value):
    high, low = split(value)
    return jnp.concatenate([high, high, low], 0)


def lane_low(shape):
    return lax.broadcasted_iota(jnp.int32, shape, len(shape) - 1) < M


def full(count):
    return [pl.BlockSpec(memory_space=VMEM)] * count


def params(collective=None, limit=56):
    return pltpu.CompilerParams(
        vmem_limit_bytes=limit << 20,
        collective_id=collective,
        has_side_effects=collective is not None,
    )


def arrived(ref, sem):
    pltpu.make_async_copy(ref, ref, sem).wait()


def send(src, dst, send_sem, recv_sem, device):
    copy = pltpu.make_async_remote_copy(
        src_ref=src,
        dst_ref=dst,
        send_sem=send_sem,
        recv_sem=recv_sem,
        device_id=device,
        device_id_type=pl.DeviceIdType.MESH,
    )
    copy.start()
    return copy


def signal(barrier, device):
    pl.semaphore_signal(
        barrier, inc=1, device_id=device, device_id_type=pl.DeviceIdType.MESH
    )


def rotation_rows(packed):
    low = lane_low(packed.shape)
    turned = pltpu.roll(packed, M, 1)
    a_low, b_low = jnp.where(low, packed, 0.0), jnp.where(low, turned, 0.0)
    a_high, b_high = jnp.where(low, 0.0, turned), jnp.where(low, 0.0, packed)
    rows = jnp.concatenate([a_low, b_low[:32], a_high, b_high[:32], b_low[32:], b_high[32:]], 0)
    high, rest = split(rows)
    cut = 2 * LANES
    return jnp.concatenate([high[:cut], rest[:cut], high[cut:], rest[cut:]], 0)


def stiff_rows(value):
    high = value.astype(BF16).astype(F32)
    blank = jnp.zeros((8, value.shape[1]), F32)
    return jnp.concatenate([high, high, value - high, blank], 0).astype(BF16)


def stiffness_band(window, stiff_ref, link_ref):
    row = lax.broadcasted_iota(jnp.int32, (LANES, LANES), 0)
    col = lax.broadcasted_iota(jnp.int32, (LANES, LANES), 1)
    far = (row - col).astype(F32)
    weight = jnp.where(row == col + 1, window[1], 0.0) + jnp.where(
        far == window[3], window[2], 0.0
    )
    both = weight + weight.T
    total = jnp.sum(both, 1, keepdims=True)
    stiff_ref[...] = jnp.where(row == col, window[0] + total, 0.0) - both
    link = jnp.sum(jnp.where(row == col, window[4], 0.0), 1, keepdims=True)
    link_ref[...] = jnp.broadcast_to(link, (LANES, LANES))
    lane = lax.broadcasted_iota(jnp.int32, (PAD, LANES), 1)

    def place(rows, inner, top, bottom):
        out = jnp.where(lane < HALF, pltpu.roll(rows, (LANES - inner) % LANES, 1), 0.0)
        out = jnp.where(
            (lane >= PAD) & (lane < PAD + REACH), pltpu.roll(rows, (LANES + PAD - top) % LANES, 1), out
        )
        at = PAD + REACH
        return jnp.where(
            (lane >= at) & (lane < at + REACH), pltpu.roll(rows, (LANES + at - bottom) % LANES, 1), out
        )

    near = stiff_ref[REACH : REACH + PAD, :]
    other = stiff_ref[REACH + HALF : REACH + HALF + PAD, :]
    near = place(near, REACH, 0, REACH + HALF)
    other = place(other, REACH + HALF, HALF, REACH + 2 * HALF)
    band = jnp.concatenate([near, other], 0)[:, : PAD + 2 * REACH]
    high = band.astype(BF16).astype(F32)
    terms = [high, band - high, high, jnp.zeros((2 * PAD, 8), F32)]
    links = jnp.where(
        lane < M, link_ref[REACH : REACH + PAD, :], link_ref[REACH + HALF : REACH + HALF + PAD, :]
    )
    return jnp.concatenate(terms, 1).astype(BF16), links


def unpack(source, rows_ref, target):
    share = 2 * HALF

    def body(i, _):
        rows = source[i]
        both = jnp.concatenate([rows, pltpu.roll(rows, M, 1)], 0)
        rows_ref[pl.ds(pl.multiple_of(i * share, 8), share), :] = both
        return 0

    lax.fori_loop(0, SPANS, body, 0, unroll=8)
    for block in range(rows_ref.shape[0] // LANES):
        cut = slice(block * LANES, (block + 1) * LANES)
        target[:, cut] = rows_ref[cut, :].T[:M]


def finish_kernel(block_ref, got_ref, ritz_in_ref, next_ref, res_ref, ritz_ref, rows_ref):
    next_ref[...] = block_ref[...]
    ritz_ref[...] = ritz_in_ref[:, :M]
    unpack(got_ref, rows_ref, res_ref)


def step_kernel(
    x_ref,
    w_ref,
    p_ref,
    coefs_refs,
    offset_ref,
    turned_ref,
    four_ref,
    back_ref,
    slots_ref,
    next_ref,
    got_res_ref,
    ritz_ref,
    pack_ref,
    got_ref,
    coef_ref,
    edge_ref,
    rot_ref,
    rall_ref,
    right_ref,
    slot_ref,
    proj_ref,
    stiff_ref,
    low_ref,
    high_ref,
    left_in_ref,
    right_in_ref,
    edge_in_ref,
    band_ref,
    link_ref,
    back_block_ref,
    back_res_ref,
    got_block_ref,
    sums_ref,
    part_ref,
    all_ref,
    rows_ref,
    sends,
    recvs,
    locals_,
):
    spans, elems = SPANS, lax.axis_size("elem")
    me, elem = lax.axis_index("span"), lax.axis_index("elem")
    ex, ez, ec = me // 16, lax.rem(me // 2, 8), lax.rem(me, 2)
    dofs = x_ref.shape[1]
    share = 2 * HALF

    up, down = me + 1, me + spans - 1
    after = {"span": lax.rem(up, spans), "elem": lax.rem(elem + up // spans, elems)}
    before = {
        "span": lax.rem(down, spans),
        "elem": lax.rem(elem + elems - 1 + down // spans, elems),
    }

    def at(x, z, c):
        return {"span": (x * 8 + z) * 2 + c}

    def elem_at(step):
        return lax.rem(elem + step, elems)

    barrier = pltpu.get_barrier_semaphore()

    def greet(step, _):
        signal(barrier, {"span": lax.rem(me + step, spans)})
        return 0

    lax.fori_loop(1, spans, greet, 0)
    for step in range(1, elems):
        signal(barrier, {"elem": elem_at(step)})
    signal(barrier, after)
    signal(barrier, before)

    rot_ref[...] = jnp.concatenate([turned_ref[:, :96], turned_ref[:, 96:]], 0).T
    own_rot = pltpu.make_async_copy(rot_ref, rall_ref.at[ex, ez, ec], locals_.at[3])
    own_rot.start()
    pl.semaphore_wait(barrier, spans - 1 + elems - 1 + 2)
    for step in range(1, 8):
        where = at(ex, lax.rem(ez + step, 8), ec)
        send(rot_ref, rall_ref.at[ex, ez, ec], sends.at[3], recvs.at[3], where)

    count = dofs // LANES
    for block in range(count):
        cut = slice(block * LANES, (block + 1) * LANES)
        pack_ref[cut, :] = jnp.concatenate([x_ref[:, cut], w_ref[:, cut]], 0).T

    def packed_at(device, number):
        row = device * share + (number % 2) * HALF + (number // 2) * dofs
        return pack_ref.at[pl.ds(row, HALF)]

    def message(q):
        number, step = q // (spans - 1), lax.rem(q, spans - 1) + 1
        other = lax.rem(me + step, spans)
        send(
            packed_at(other, number),
            got_ref.at[pl.ds(number * HALF, HALF), me],
            sends.at[number],
            recvs.at[number],
            {"span": other},
        )

    def messages(first, last):
        def body(q, _):
            message(q)
            return 0

        lax.fori_loop(first, last, body, 0)

    rest_z, rest_x = rall_ref.at[0, pl.ds(0, 7), 0], rall_ref.at[pl.ds(0, 3), :, 0]
    rest_c = rall_ref.at[:, :, 0]
    messages(0, spans - 1)
    own_rot.wait()
    arrived(rest_z, recvs.at[3])
    for step in range(1, 4):
        mine = rall_ref.at[ex, :, ec]
        send(mine, mine, sends.at[4], recvs.at[4], at(lax.rem(ex + step, 4), ez, ec))
    messages(spans - 1, 2 * (spans - 1))
    p = p_ref[...]
    moved = pltpu.roll(p, dofs - HALF, 1)
    for block in range(count):
        cut = slice(block * LANES, (block + 1) * LANES)
        below = slice(dofs + block * LANES, dofs + (block + 1) * LANES)
        pack_ref[below, :] = jnp.concatenate([p[:, cut], moved[:, cut]], 0).T
    messages(2 * (spans - 1), 3 * (spans - 1))
    own = []
    for number in range(3):
        target = got_ref.at[pl.ds(number * HALF, HALF), me]
        own.append(pltpu.make_async_copy(packed_at(me, number), target, locals_.at[number]))
        own[number].start()

    ground_ref, tension_ref, dropper_ref, link_in_ref = coefs_refs
    grid = (count, LANES)
    position = elem * dofs + LANES * lax.broadcasted_iota(jnp.int32, grid, 0)
    position = position + lax.broadcasted_iota(jnp.int32, grid, 1)
    offset = offset_ref[...]
    values = [
        ground_ref[...],
        jnp.where(position < dofs * elems - 1, tension_ref[...], 0.0),
        jnp.where(position + offset < dofs * elems, dropper_ref[...], 0.0),
        offset.astype(F32),
        link_in_ref[...],
    ]
    coef_ref[...] = jnp.zeros_like(coef_ref)
    edge_ref[...] = jnp.zeros_like(edge_ref)
    for number, value in enumerate(values):
        coef_ref[number, 1 : 1 + count, :] = value
        edge_ref[number : number + 1, :] = value[count - 1 :]
    edge = send(edge_ref, edge_in_ref, sends.at[6], recvs.at[6], {"elem": elem_at(1)})

    slot_ref[...] = jnp.zeros_like(slot_ref)

    edge.wait()
    for number in range(5):
        coef_ref[number, 0:1, :] = edge_in_ref[number : number + 1, :]
    start = LANES - REACH + me * share
    row, kept_lanes = start // LANES, LANES - lax.rem(start, LANES)
    turn = lax.rem(kept_lanes, LANES)
    lane = lax.broadcasted_iota(jnp.int32, (1, LANES), 1)
    window = []
    for number in range(5):
        one = pltpu.roll(coef_ref[number, pl.ds(row, 1), :], turn, 1)
        two = pltpu.roll(coef_ref[number, pl.ds(row + 1, 1), :], turn, 1)
        window.append(jnp.where(lane < kept_lanes, one, two))
    band, links = stiffness_band(window, band_ref, link_ref)
    arrived(rest_x, recvs.at[4])
    mine = rall_ref.at[:, :, ec]
    cross = send(mine, mine, sends.at[5], recvs.at[5], at(ex, ez, 1 - ec))

    def prepare(core):
        def body(step, _):
            rows = rotation_rows(rall_ref[step // 8, lax.rem(step, 8), core])
            right_ref[2 * step + core] = rows
            return 0

        lax.fori_loop(0, spans // 2, body, 0, unroll=8)

    prepare(ec)

    def transform(number):
        own[number].wait()
        arrived(got_ref.at[pl.ds(0, HALF), pl.ds(0, spans - 1)], recvs.at[number])
        group = 4

        def body(step, _):
            rows = jnp.concatenate(
                [got_ref[number * HALF + step * group + q] for q in range(group)], 1
            )
            out = jnp.dot(four_ref[...], right_rows(rows), preferred_element_type=F32)
            for q in range(group):
                slot_ref[number, pl.ds(step * group + q, spans, stride=PAD), :] = out[
                    :, q * LANES : (q + 1) * LANES
                ]
            return 0

        lax.fori_loop(0, HALF // group, body, 0, unroll=5)

    def product(j, numbers, first, last):
        cut = pl.ds(pl.multiple_of(j * PAD, 8), PAD)
        rows = jnp.concatenate([slot_ref[number, cut, :] for number in numbers], 1)
        high = rows.astype(BF16).astype(F32)
        left = jnp.concatenate([high, rows - high], 0).astype(BF16)
        out = jnp.dot(
            jnp.concatenate([left, left], 1),
            right_ref[j, first:last],
            preferred_element_type=F32,
        )
        return cut, out[:PAD] + out[PAD:]

    def rotate_first(step, _, core):
        cut, out = product(2 * step + core, (0, 1), 0, 4 * LANES)
        proj_ref[cut, :] = out
        return 0

    def rotate_last(j, _):
        cut, out = product(j, (2,), 4 * LANES, 6 * LANES)
        out = out + proj_ref[cut, :]
        proj_ref[cut, :] = out
        low_ref[j] = out[:REACH]
        high_ref[j] = out[HALF - REACH : HALF]
        return 0

    transform(0)
    transform(1)
    lax.fori_loop(0, spans // 2, functools.partial(rotate_first, core=ec), 0, unroll=8)
    cross.wait_recv()
    prepare(1 - ec)
    lax.fori_loop(0, spans // 2, functools.partial(rotate_first, core=1 - ec), 0, unroll=8)
    transform(2)
    lax.fori_loop(0, spans, rotate_last, 0, unroll=8)
    halo = [
        send(high_ref, left_in_ref, sends.at[7], recvs.at[7], after),
        send(low_ref, right_in_ref, sends.at[8], recvs.at[8], before),
    ]

    def inverse(source, target):
        group = 4

        def body(step, _):
            rows = [source(pl.ds(step * group + q, spans, stride=PAD)) for q in range(group)]
            out = jnp.dot(
                back_ref[...], right_rows(jnp.concatenate(rows, 1)), preferred_element_type=F32
            )
            for q in range(group):
                target[step * group + q] = out[:, q * LANES : (q + 1) * LANES]
            return 0

        lax.fori_loop(0, HALF // group, body, 0, unroll=5)

    def give_back(source, target, number, first, last):
        def body(step, _):
            other = lax.rem(me + step, spans)
            send(
                source.at[:, other],
                target.at[me],
                sends.at[number],
                recvs.at[number],
                {"span": other},
            )
            return 0

        lax.fori_loop(first, last, body, 0)

    def give_block(first, last):
        give_back(back_block_ref, got_block_ref, 9, first, last)

    inverse(lambda rows: proj_ref[rows, :], back_block_ref)
    own_block = pltpu.make_async_copy(
        back_block_ref.at[:, me], got_block_ref.at[me], locals_.at[9]
    )
    own_block.start()

    for copy in halo:
        copy.wait()
    half = lane_low((REACH, LANES))
    low = lane_low((PAD, LANES))
    kept = lax.broadcasted_iota(jnp.int32, (PAD, LANES), 0) < HALF
    side = lane_low((1, LANES))

    def stiffen(step, _):
        group = 4
        parts = []
        for q in range(group):
            j = step * group + q
            rows = proj_ref[pl.ds(pl.multiple_of(j * PAD, 8), PAD), :]
            top = pltpu.roll(jnp.where(half, high_ref[j], left_in_ref[j]), M, 1)
            bottom = pltpu.roll(jnp.where(half, right_in_ref[j], low_ref[j]), M, 1)
            parts.append(jnp.concatenate([rows, top, bottom], 0))
        out = jnp.dot(
            band, stiff_rows(jnp.concatenate(parts, 1)), preferred_element_type=F32
        )
        for q in range(group):
            j = step * group + q
            cut = slice(q * LANES, (q + 1) * LANES)
            rows = parts[q][:PAD]
            stiff = jnp.where(low, out[:PAD, cut], out[PAD:, cut])
            stiff = stiff + slots_ref[pl.ds(j, 1), :] * links * rows
            stiff_ref[pl.ds(pl.multiple_of(j * PAD, 8), PAD), :] = stiff
            energy = jnp.sum(jnp.where(kept, rows * stiff, 0.0), 0, keepdims=True)
            weight = jnp.sum(jnp.where(kept, rows * rows, 0.0), 0, keepdims=True)
            energy = energy + pltpu.roll(energy, M, 1)
            weight = weight + pltpu.roll(weight, M, 1)
            sums_ref[pl.ds(j, 1), :] = jnp.where(side, energy, weight)
        return 0

    lax.fori_loop(0, spans // 4, stiffen, 0, unroll=8)

    rest = pl.ds(0, 7)
    part_ref[0, elem] = sums_ref[pl.ds(pl.multiple_of(elem * 8, 8), 8), :]
    for step in range(1, elems):
        other = elem_at(step)
        send(
            sums_ref.at[pl.ds(other * 8, 8)],
            part_ref.at[0, elem],
            sends.at[10],
            recvs.at[10],
            {"elem": other},
        )
    give_block(1, 22)
    arrived(part_ref.at[0, rest], recvs.at[10])
    part_ref[1, ez] = jnp.sum(part_ref[0], 0)
    for step in range(1, 8):
        where = at(ex, lax.rem(ez + step, 8), ec)
        send(part_ref.at[1, ez], part_ref.at[1, ez], sends.at[11], recvs.at[11], where)
    give_block(22, 43)
    arrived(part_ref.at[1, rest], recvs.at[11])
    pair = ex * 2 + ec
    part_ref[2, pair] = jnp.sum(part_ref[1], 0)
    for step in range(1, 8):
        other = lax.rem(pair + step, 8)
        where = at(other // 2, ez, lax.rem(other, 2))
        send(part_ref.at[2, pair], part_ref.at[2, pair], sends.at[12], recvs.at[12], where)
    give_block(43, 64)
    arrived(part_ref.at[2, rest], recvs.at[12])
    total = jnp.sum(part_ref[2], 0)
    ritz = total / (pltpu.roll(total, M, 1) + 1e-06)
    ritz = jnp.where(lane_low((8, LANES)), ritz, pltpu.roll(ritz, M, 1))
    all_ref[elem] = ritz
    for step in range(1, elems):
        send(
            all_ref.at[elem], all_ref.at[elem], sends.at[13], recvs.at[13], {"elem": elem_at(step)}
        )
    arrived(all_ref.at[rest], recvs.at[13])
    ritz = jnp.concatenate([all_ref[g] for g in range(8)], 0)
    sums = lax.broadcasted_iota(jnp.int32, ritz.shape, 0) == me
    ritz_ref[...] = jnp.sum(jnp.where(sums, ritz, 0.0), 0, keepdims=True)

    inverse(lambda rows: stiff_ref[rows, :] - ritz * proj_ref[rows, :], back_res_ref)
    own_res = pltpu.make_async_copy(back_res_ref.at[:, me], got_res_ref.at[me], locals_.at[14])
    own_res.start()
    give_back(back_res_ref, got_res_ref, 14, 1, spans)

    rest = pl.ds(0, spans - 1)
    own_block.wait()
    arrived(got_block_ref.at[rest], recvs.at[9])
    unpack(got_block_ref, rows_ref, next_ref)
    own_res.wait()
    arrived(got_res_ref.at[rest], recvs.at[14])

    for number in range(3):
        arrived(got_ref.at[pl.ds(0, HALF), rest], sends.at[number])
    arrived(rest_z, sends.at[3])
    arrived(rest_x, sends.at[4])
    arrived(rest_c, sends.at[5])
    arrived(got_block_ref.at[rest], sends.at[9])
    for stage in range(3):
        arrived(part_ref.at[stage, pl.ds(0, 7)], sends.at[10 + stage])
    arrived(all_ref.at[pl.ds(0, 7)], sends.at[13])
    arrived(got_res_ref.at[rest], sends.at[14])


def shape(*dims):
    return jax.ShapeDtypeStruct(dims, F32)


def on_device(
    current_block,
    search_block,
    previous_block,
    ground_spring,
    wire_tension,
    dropper_stiff,
    dropper_offset,
    span_link,
    ritz_rotation,
):
    dofs = current_block.shape[2]
    spans = lax.axis_size("span")
    share = dofs // spans
    matrix, links = fourier_np(spans)

    grid = (dofs // LANES, LANES)
    rows = spans * PAD
    slots = jnp.asarray(np.repeat(links[:, None], LANES, 1).astype(np.float32))

    block, got, ritz = pl.pallas_call(
        step_kernel,
        out_shape=(shape(M, dofs), shape(spans, HALF, LANES), shape(1, LANES)),
        in_specs=full(3) + [full(4)] + full(5),
        out_specs=tuple(full(3)),
        scratch_shapes=[
            VMEM((2 * dofs, LANES), F32),
            VMEM((3 * HALF, spans, LANES), F32),
            VMEM((5, 24, LANES), F32),
            VMEM((8, LANES), F32),
            VMEM((96, LANES), F32),
            VMEM((4, 8, 2, 96, LANES), F32),
            VMEM((spans, 768, LANES), BF16),
            VMEM((3, rows, LANES), F32),
            VMEM((rows, LANES), F32),
            VMEM((rows, LANES), F32),
            VMEM((spans, REACH, LANES), F32),
            VMEM((spans, REACH, LANES), F32),
            VMEM((spans, REACH, LANES), F32),
            VMEM((spans, REACH, LANES), F32),
            VMEM((8, LANES), F32),
            VMEM((LANES, LANES), F32),
            VMEM((LANES, LANES), F32),
            VMEM((HALF, spans, LANES), F32),
            VMEM((HALF, spans, LANES), F32),
            VMEM((spans, HALF, LANES), F32),
            VMEM((spans, LANES), F32),
            VMEM((3, 8, 8, LANES), F32),
            VMEM((8, 8, LANES), F32),
            VMEM((dofs, LANES), F32),
            pltpu.SemaphoreType.DMA((15,)),
            pltpu.SemaphoreType.DMA((15,)),
            pltpu.SemaphoreType.DMA((15,)),
        ],
        compiler_params=params(0),
    )(
        current_block[0],
        search_block[0],
        previous_block[0],
        [
            coef.reshape(grid)
            for coef in (ground_spring, wire_tension, dropper_stiff, span_link)
        ],
        dropper_offset.reshape(grid),
        ritz_rotation[0].T,
        jnp.asarray(left_terms(matrix)),
        jnp.asarray(left_terms(matrix.T)),
        slots,
    )
    next_block, next_residual, ritz = pl.pallas_call(
        finish_kernel,
        out_shape=(shape(M, dofs), shape(M, dofs), shape(1, M)),
        in_specs=full(3),
        out_specs=tuple(full(3)),
        scratch_shapes=[VMEM((dofs, LANES), F32)],
        compiler_params=params(limit=60),
    )(block, got, ritz)
    return (next_block[None], next_residual[None], ritz)


def solution(mesh):
    return jax.shard_map(
        on_device,
        mesh=mesh,
        in_specs=(
            P("span", None, "elem"),
            P("span", None, "elem"),
            P("span", None, "elem"),
            P("elem"),
            P("elem"),
            P("elem"),
            P("elem"),
            P("elem"),
            P("span", None, None),
        ),
        out_specs=(P("span", None, "elem"), P("span", None, "elem"), P("span", None)),
        check_vma=False,
    )
```

```python
import functools
import math

import jax
import jax.numpy as jnp
import ml_dtypes
import numpy as np
from jax import lax
from jax.experimental import pallas as pl
from jax.experimental.pallas import tpu as pltpu
from jax.sharding import PartitionSpec as P

REACH = 8
SPANS = 64
M = 64
HALF = 20
PAD = 24
LANES = 128
F32 = jnp.float32
BF16 = jnp.bfloat16
VMEM = pltpu.VMEM


def split_np(matrix):
    high = matrix.astype(np.float32).astype(ml_dtypes.bfloat16)
    low = (matrix - high.astype(np.float64)).astype(ml_dtypes.bfloat16)
    return high, low


def fourier_np(count):
    half = count // 2
    row = np.arange(count)[:, None]
    col = np.arange(count)[None, :]
    wave = np.where(row <= half, row, row - half)
    phase = (wave * col % count) * (2.0 * math.pi / count)
    scaled = np.where(row <= half, np.cos(phase), np.sin(phase)) * math.sqrt(2.0 / count)
    edge = (row == 0) | (row == half)
    matrix = np.where(edge, np.cos(phase) * math.sqrt(1.0 / count), scaled)
    slots = np.arange(count)
    slot_wave = np.where(slots <= half, slots, slots - half)
    links = 2.0 * (1.0 - np.cos(slot_wave * (2.0 * math.pi / count)))
    return matrix, links


def left_terms(matrix):
    high, low = split_np(matrix)
    return np.concatenate([high, low, high], 1)


def split(value):
    high = value.astype(BF16)
    low = (value - high.astype(F32)).astype(BF16)
    return high, low


def right_rows(value):
    high, low = split(value)
    return jnp.concatenate([high, high, low], 0)


def lane_low(shape):
    return lax.broadcasted_iota(jnp.int32, shape, len(shape) - 1) < M


def full(count):
    return [pl.BlockSpec(memory_space=VMEM)] * count


def params(collective=None, limit=56):
    return pltpu.CompilerParams(
        vmem_limit_bytes=limit << 20,
        collective_id=collective,
        has_side_effects=collective is not None,
    )


def arrived(ref, sem):
    pltpu.make_async_copy(ref, ref, sem).wait()


def send(src, dst, send_sem, recv_sem, device):
    copy = pltpu.make_async_remote_copy(
        src_ref=src,
        dst_ref=dst,
        send_sem=send_sem,
        recv_sem=recv_sem,
        device_id=device,
        device_id_type=pl.DeviceIdType.MESH,
    )
    copy.start()
    return copy


def signal(barrier, device):
    pl.semaphore_signal(
        barrier, inc=1, device_id=device, device_id_type=pl.DeviceIdType.MESH
    )


def rotation_rows(packed):
    low = lane_low(packed.shape)
    turned = pltpu.roll(packed, M, 1)
    a_low, b_low = jnp.where(low, packed, 0.0), jnp.where(low, turned, 0.0)
    a_high, b_high = jnp.where(low, 0.0, turned), jnp.where(low, 0.0, packed)
    rows = jnp.concatenate([a_low, b_low[:32], a_high, b_high[:32], b_low[32:], b_high[32:]], 0)
    high, rest = split(rows)
    cut = 2 * LANES
    return jnp.concatenate([high[:cut], rest[:cut], high[cut:], rest[cut:]], 0)


def stiff_rows(value):
    high = value.astype(BF16).astype(F32)
    blank = jnp.zeros((8, value.shape[1]), F32)
    return jnp.concatenate([high, high, value - high, blank], 0).astype(BF16)


def stiffness_band(window, stiff_ref, link_ref):
    row = lax.broadcasted_iota(jnp.int32, (LANES, LANES), 0)
    col = lax.broadcasted_iota(jnp.int32, (LANES, LANES), 1)
    far = (row - col).astype(F32)
    weight = jnp.where(row == col + 1, window[1], 0.0) + jnp.where(
        far == window[3], window[2], 0.0
    )
    both = weight + weight.T
    total = jnp.sum(both, 1, keepdims=True)
    stiff_ref[...] = jnp.where(row == col, window[0] + total, 0.0) - both
    link = jnp.sum(jnp.where(row == col, window[4], 0.0), 1, keepdims=True)
    link_ref[...] = jnp.broadcast_to(link, (LANES, LANES))
    lane = lax.broadcasted_iota(jnp.int32, (PAD, LANES), 1)

    def place(rows, inner, top, bottom):
        out = jnp.where(lane < HALF, pltpu.roll(rows, (LANES - inner) % LANES, 1), 0.0)
        out = jnp.where(
            (lane >= PAD) & (lane < PAD + REACH), pltpu.roll(rows, (LANES + PAD - top) % LANES, 1), out
        )
        at = PAD + REACH
        return jnp.where(
            (lane >= at) & (lane < at + REACH), pltpu.roll(rows, (LANES + at - bottom) % LANES, 1), out
        )

    near = stiff_ref[REACH : REACH + PAD, :]
    other = stiff_ref[REACH + HALF : REACH + HALF + PAD, :]
    near = place(near, REACH, 0, REACH + HALF)
    other = place(other, REACH + HALF, HALF, REACH + 2 * HALF)
    band = jnp.concatenate([near, other], 0)[:, : PAD + 2 * REACH]
    high = band.astype(BF16).astype(F32)
    terms = [high, band - high, high, jnp.zeros((2 * PAD, 8), F32)]
    links = jnp.where(
        lane < M, link_ref[REACH : REACH + PAD, :], link_ref[REACH + HALF : REACH + HALF + PAD, :]
    )
    return jnp.concatenate(terms, 1).astype(BF16), links


def unpack(source, rows_ref, target):
    share = 2 * HALF

    def body(i, _):
        rows = source[i]
        both = jnp.concatenate([rows, pltpu.roll(rows, M, 1)], 0)
        rows_ref[pl.ds(pl.multiple_of(i * share, 8), share), :] = both
        return 0

    lax.fori_loop(0, SPANS, body, 0, unroll=8)
    for block in range(rows_ref.shape[0] // LANES):
        cut = slice(block * LANES, (block + 1) * LANES)
        target[:, cut] = rows_ref[cut, :].T[:M]


def finish_kernel(block_ref, got_ref, ritz_in_ref, next_ref, res_ref, ritz_ref, rows_ref):
    next_ref[...] = block_ref[...]
    ritz_ref[...] = ritz_in_ref[:, :M]
    unpack(got_ref, rows_ref, res_ref)


def step_kernel(
    x_in_ref,
    w_in_ref,
    p_in_ref,
    coefs_refs,
    offset_ref,
    turned_ref,
    four_ref,
    back_ref,
    slots_ref,
    next_out_ref,
    got_res_ref,
    ritz_ref,
    x_ref,
    w_ref,
    p_ref,
    next_ref,
    pack_ref,
    got_ref,
    coef_ref,
    edge_ref,
    rot_ref,
    rall_ref,
    right_ref,
    slot_ref,
    proj_ref,
    stiff_ref,
    low_ref,
    high_ref,
    left_in_ref,
    right_in_ref,
    edge_in_ref,
    band_ref,
    link_ref,
    back_block_ref,
    back_res_ref,
    got_block_ref,
    sums_ref,
    part_ref,
    all_ref,
    rows_ref,
    sends,
    recvs,
    locals_,
):
    spans, elems = SPANS, lax.axis_size("elem")
    me, elem = lax.axis_index("span"), lax.axis_index("elem")
    ex, ez, ec = me // 16, lax.rem(me // 2, 8), lax.rem(me, 2)
    dofs = x_in_ref.shape[1]
    share = 2 * HALF

    up, down = me + 1, me + spans - 1
    after = {"span": lax.rem(up, spans), "elem": lax.rem(elem + up // spans, elems)}
    before = {
        "span": lax.rem(down, spans),
        "elem": lax.rem(elem + elems - 1 + down // spans, elems),
    }

    def at(x, z, c):
        return {"span": (x * 8 + z) * 2 + c}

    def elem_at(step):
        return lax.rem(elem + step, elems)

    barrier = pltpu.get_barrier_semaphore()

    def greet(step, _):
        signal(barrier, {"span": lax.rem(me + step, spans)})
        return 0

    loads = [
        pltpu.make_async_copy(source, target, locals_.at[number])
        for number, (source, target) in enumerate(
            ((x_in_ref, x_ref), (w_in_ref, w_ref), (p_in_ref, p_ref)), 4
        )
    ]
    for copy in loads:
        copy.start()
    lax.fori_loop(1, spans, greet, 0, unroll=7)
    for step in range(1, elems):
        signal(barrier, {"elem": elem_at(step)})
    signal(barrier, after)
    signal(barrier, before)

    rot_ref[...] = jnp.concatenate([turned_ref[:, :96], turned_ref[:, 96:]], 0).T
    own_rot = pltpu.make_async_copy(rot_ref, rall_ref.at[ex, ez, ec], locals_.at[3])
    own_rot.start()
    pl.semaphore_wait(barrier, spans - 1 + elems - 1 + 2)
    for step in range(1, 8):
        where = at(ex, lax.rem(ez + step, 8), ec)
        send(rot_ref, rall_ref.at[ex, ez, ec], sends.at[3], recvs.at[3], where)

    for copy in loads:
        copy.wait()
    count = dofs // LANES
    for block in range(count):
        cut = slice(block * LANES, (block + 1) * LANES)
        pack_ref[cut, :] = jnp.concatenate([x_ref[:, cut], w_ref[:, cut]], 0).T

    def packed_at(device, number):
        row = device * share + (number % 2) * HALF + (number // 2) * dofs
        return pack_ref.at[pl.ds(row, HALF)]

    def message(q):
        number, step = q // (spans - 1), lax.rem(q, spans - 1) + 1
        other = lax.rem(me + step, spans)
        send(
            packed_at(other, number),
            got_ref.at[pl.ds(number * HALF, HALF), me],
            sends.at[number],
            recvs.at[number],
            {"span": other},
        )

    def messages(first, last):
        def body(q, _):
            message(q)
            return 0

        lax.fori_loop(first, last, body, 0)

    rest_z, rest_x = rall_ref.at[0, pl.ds(0, 7), 0], rall_ref.at[pl.ds(0, 3), :, 0]
    rest_c = rall_ref.at[:, :, 0]
    messages(0, spans - 1)
    own_rot.wait()
    arrived(rest_z, recvs.at[3])
    for step in range(1, 4):
        mine = rall_ref.at[ex, :, ec]
        send(mine, mine, sends.at[4], recvs.at[4], at(lax.rem(ex + step, 4), ez, ec))
    messages(spans - 1, 2 * (spans - 1))
    p = p_ref[...]
    moved = pltpu.roll(p, dofs - HALF, 1)
    for block in range(count):
        cut = slice(block * LANES, (block + 1) * LANES)
        below = slice(dofs + block * LANES, dofs + (block + 1) * LANES)
        pack_ref[below, :] = jnp.concatenate([p[:, cut], moved[:, cut]], 0).T
    messages(2 * (spans - 1), 3 * (spans - 1))
    own = []
    for number in range(3):
        target = got_ref.at[pl.ds(number * HALF, HALF), me]
        own.append(pltpu.make_async_copy(packed_at(me, number), target, locals_.at[number]))
        own[number].start()

    ground_ref, tension_ref, dropper_ref, link_in_ref = coefs_refs
    grid = (count, LANES)
    position = elem * dofs + LANES * lax.broadcasted_iota(jnp.int32, grid, 0)
    position = position + lax.broadcasted_iota(jnp.int32, grid, 1)
    offset = offset_ref[...]
    values = [
        ground_ref[...],
        jnp.where(position < dofs * elems - 1, tension_ref[...], 0.0),
        jnp.where(position + offset < dofs * elems, dropper_ref[...], 0.0),
        offset.astype(F32),
        link_in_ref[...],
    ]
    coef_ref[...] = jnp.zeros_like(coef_ref)
    edge_ref[...] = jnp.zeros_like(edge_ref)
    for number, value in enumerate(values):
        coef_ref[number, 1 : 1 + count, :] = value
        edge_ref[number : number + 1, :] = value[count - 1 :]
    edge = send(edge_ref, edge_in_ref, sends.at[6], recvs.at[6], {"elem": elem_at(1)})

    slot_ref[...] = jnp.zeros_like(slot_ref)

    edge.wait()
    for number in range(5):
        coef_ref[number, 0:1, :] = edge_in_ref[number : number + 1, :]
    start = LANES - REACH + me * share
    row, kept_lanes = start // LANES, LANES - lax.rem(start, LANES)
    turn = lax.rem(kept_lanes, LANES)
    lane = lax.broadcasted_iota(jnp.int32, (1, LANES), 1)
    window = []
    for number in range(5):
        one = pltpu.roll(coef_ref[number, pl.ds(row, 1), :], turn, 1)
        two = pltpu.roll(coef_ref[number, pl.ds(row + 1, 1), :], turn, 1)
        window.append(jnp.where(lane < kept_lanes, one, two))
    band, links = stiffness_band(window, band_ref, link_ref)
    arrived(rest_x, recvs.at[4])
    mine = rall_ref.at[:, :, ec]
    cross = send(mine, mine, sends.at[5], recvs.at[5], at(ex, ez, 1 - ec))

    def prepare(core):
        def body(step, _):
            rows = rotation_rows(rall_ref[step // 8, lax.rem(step, 8), core])
            right_ref[2 * step + core] = rows
            return 0

        lax.fori_loop(0, spans // 2, body, 0, unroll=8)

    prepare(ec)

    def transform(number):
        own[number].wait()
        arrived(got_ref.at[pl.ds(0, HALF), pl.ds(0, spans - 1)], recvs.at[number])
        group = 4

        def body(step, _):
            rows = jnp.concatenate(
                [got_ref[number * HALF + step * group + q] for q in range(group)], 1
            )
            out = jnp.dot(four_ref[...], right_rows(rows), preferred_element_type=F32)
            for q in range(group):
                slot_ref[number, pl.ds(step * group + q, spans, stride=PAD), :] = out[
                    :, q * LANES : (q + 1) * LANES
                ]
            return 0

        lax.fori_loop(0, HALF // group, body, 0, unroll=5)

    def product(j, numbers, first, last):
        cut = pl.ds(pl.multiple_of(j * PAD, 8), PAD)
        rows = jnp.concatenate([slot_ref[number, cut, :] for number in numbers], 1)
        high = rows.astype(BF16).astype(F32)
        left = jnp.concatenate([high, rows - high], 0).astype(BF16)
        out = jnp.dot(
            jnp.concatenate([left, left], 1),
            right_ref[j, first:last],
            preferred_element_type=F32,
        )
        return cut, out[:PAD] + out[PAD:]

    def rotate_first(step, _, core):
        cut, out = product(2 * step + core, (0, 1), 0, 4 * LANES)
        proj_ref[cut, :] = out
        return 0

    def rotate_last(j, _):
        cut, out = product(j, (2,), 4 * LANES, 6 * LANES)
        out = out + proj_ref[cut, :]
        proj_ref[cut, :] = out
        low_ref[j] = out[:REACH]
        high_ref[j] = out[HALF - REACH : HALF]
        return 0

    transform(0)
    transform(1)
    lax.fori_loop(0, spans // 2, functools.partial(rotate_first, core=ec), 0, unroll=8)
    cross.wait_recv()
    prepare(1 - ec)
    lax.fori_loop(0, spans // 2, functools.partial(rotate_first, core=1 - ec), 0, unroll=8)
    transform(2)
    lax.fori_loop(0, spans, rotate_last, 0, unroll=8)
    halo = [
        send(high_ref, left_in_ref, sends.at[7], recvs.at[7], after),
        send(low_ref, right_in_ref, sends.at[8], recvs.at[8], before),
    ]

    def inverse(source, target):
        group = 4

        def body(step, _):
            rows = [source(pl.ds(step * group + q, spans, stride=PAD)) for q in range(group)]
            out = jnp.dot(
                back_ref[...], right_rows(jnp.concatenate(rows, 1)), preferred_element_type=F32
            )
            for q in range(group):
                target[step * group + q] = out[:, q * LANES : (q + 1) * LANES]
            return 0

        lax.fori_loop(0, HALF // group, body, 0, unroll=5)

    def give_back(source, target, number, first, last):
        def body(step, _):
            other = lax.rem(me + step, spans)
            send(
                source.at[:, other],
                target.at[me],
                sends.at[number],
                recvs.at[number],
                {"span": other},
            )
            return 0

        lax.fori_loop(first, last, body, 0)

    def give_block(first, last):
        give_back(back_block_ref, got_block_ref, 9, first, last)

    inverse(lambda rows: proj_ref[rows, :], back_block_ref)
    own_block = pltpu.make_async_copy(
        back_block_ref.at[:, me], got_block_ref.at[me], locals_.at[9]
    )
    own_block.start()

    for copy in halo:
        copy.wait()
    half = lane_low((REACH, LANES))
    low = lane_low((PAD, LANES))
    kept = lax.broadcasted_iota(jnp.int32, (PAD, LANES), 0) < HALF
    side = lane_low((1, LANES))

    def stiffen(step, _):
        group = 4
        parts = []
        for q in range(group):
            j = step * group + q
            rows = proj_ref[pl.ds(pl.multiple_of(j * PAD, 8), PAD), :]
            top = pltpu.roll(jnp.where(half, high_ref[j], left_in_ref[j]), M, 1)
            bottom = pltpu.roll(jnp.where(half, right_in_ref[j], low_ref[j]), M, 1)
            parts.append(jnp.concatenate([rows, top, bottom], 0))
        out = jnp.dot(
            band, stiff_rows(jnp.concatenate(parts, 1)), preferred_element_type=F32
        )
        for q in range(group):
            j = step * group + q
            cut = slice(q * LANES, (q + 1) * LANES)
            rows = parts[q][:PAD]
            stiff = jnp.where(low, out[:PAD, cut], out[PAD:, cut])
            stiff = stiff + slots_ref[pl.ds(j, 1), :] * links * rows
            stiff_ref[pl.ds(pl.multiple_of(j * PAD, 8), PAD), :] = stiff
            energy = jnp.sum(jnp.where(kept, rows * stiff, 0.0), 0, keepdims=True)
            weight = jnp.sum(jnp.where(kept, rows * rows, 0.0), 0, keepdims=True)
            energy = energy + pltpu.roll(energy, M, 1)
            weight = weight + pltpu.roll(weight, M, 1)
            sums_ref[pl.ds(j, 1), :] = jnp.where(side, energy, weight)
        return 0

    lax.fori_loop(0, spans // 4, stiffen, 0, unroll=8)

    rest = pl.ds(0, 7)
    part_ref[0, elem] = sums_ref[pl.ds(pl.multiple_of(elem * 8, 8), 8), :]
    for step in range(1, elems):
        other = elem_at(step)
        send(
            sums_ref.at[pl.ds(other * 8, 8)],
            part_ref.at[0, elem],
            sends.at[10],
            recvs.at[10],
            {"elem": other},
        )
    give_block(1, 22)
    arrived(part_ref.at[0, rest], recvs.at[10])
    part_ref[1, ez] = jnp.sum(part_ref[0], 0)
    for step in range(1, 8):
        where = at(ex, lax.rem(ez + step, 8), ec)
        send(part_ref.at[1, ez], part_ref.at[1, ez], sends.at[11], recvs.at[11], where)
    give_block(22, 43)
    arrived(part_ref.at[1, rest], recvs.at[11])
    pair = ex * 2 + ec
    part_ref[2, pair] = jnp.sum(part_ref[1], 0)
    for step in range(1, 8):
        other = lax.rem(pair + step, 8)
        where = at(other // 2, ez, lax.rem(other, 2))
        send(part_ref.at[2, pair], part_ref.at[2, pair], sends.at[12], recvs.at[12], where)
    give_block(43, 64)
    arrived(part_ref.at[2, rest], recvs.at[12])
    total = jnp.sum(part_ref[2], 0)
    ritz = total / (pltpu.roll(total, M, 1) + 1e-06)
    ritz = jnp.where(lane_low((8, LANES)), ritz, pltpu.roll(ritz, M, 1))
    all_ref[elem] = ritz
    for step in range(1, elems):
        send(
            all_ref.at[elem], all_ref.at[elem], sends.at[13], recvs.at[13], {"elem": elem_at(step)}
        )
    arrived(all_ref.at[rest], recvs.at[13])
    ritz = jnp.concatenate([all_ref[g] for g in range(8)], 0)
    sums = lax.broadcasted_iota(jnp.int32, ritz.shape, 0) == me
    ritz_ref[...] = jnp.sum(jnp.where(sums, ritz, 0.0), 0, keepdims=True)

    inverse(lambda rows: stiff_ref[rows, :] - ritz * proj_ref[rows, :], back_res_ref)
    own_res = pltpu.make_async_copy(back_res_ref.at[:, me], got_res_ref.at[me], locals_.at[14])
    own_res.start()
    give_back(back_res_ref, got_res_ref, 14, 1, spans)

    rest = pl.ds(0, spans - 1)
    own_block.wait()
    arrived(got_block_ref.at[rest], recvs.at[9])
    unpack(got_block_ref, rows_ref, next_ref)
    leave = pltpu.make_async_copy(next_ref, next_out_ref, locals_.at[7])
    leave.start()
    own_res.wait()
    arrived(got_res_ref.at[rest], recvs.at[14])

    for number in range(3):
        arrived(got_ref.at[pl.ds(0, HALF), rest], sends.at[number])
    arrived(rest_z, sends.at[3])
    arrived(rest_x, sends.at[4])
    arrived(rest_c, sends.at[5])
    arrived(got_block_ref.at[rest], sends.at[9])
    for stage in range(3):
        arrived(part_ref.at[stage, pl.ds(0, 7)], sends.at[10 + stage])
    arrived(all_ref.at[pl.ds(0, 7)], sends.at[13])
    arrived(got_res_ref.at[rest], sends.at[14])
    leave.wait()


def shape(*dims):
    return jax.ShapeDtypeStruct(dims, F32)


def on_device(
    current_block,
    search_block,
    previous_block,
    ground_spring,
    wire_tension,
    dropper_stiff,
    dropper_offset,
    span_link,
    ritz_rotation,
):
    dofs = current_block.shape[2]
    spans = lax.axis_size("span")
    share = dofs // spans
    matrix, links = fourier_np(spans)

    grid = (dofs // LANES, LANES)
    rows = (spans + 1) * PAD
    slots = jnp.asarray(np.repeat(links[:, None], LANES, 1).astype(np.float32))

    anywhere = pl.BlockSpec(memory_space=pl.ANY)

    block, got, ritz = pl.pallas_call(
        step_kernel,
        out_shape=(shape(M, dofs), shape(spans, HALF, LANES), shape(1, LANES)),
        in_specs=[anywhere] * 3 + [full(4)] + full(5),
        out_specs=(anywhere,) + tuple(full(2)),
        scratch_shapes=[
            VMEM((M, dofs), F32),
            VMEM((M, dofs), F32),
            VMEM((M, dofs), F32),
            VMEM((M, dofs), F32),
            VMEM((2 * dofs, LANES), F32),
            VMEM((3 * HALF, spans, LANES), F32),
            VMEM((5, 24, LANES), F32),
            VMEM((8, LANES), F32),
            VMEM((96, LANES), F32),
            VMEM((4, 8, 2, 96, LANES), F32),
            VMEM((spans, 768, LANES), BF16),
            VMEM((3, rows, LANES), F32),
            VMEM((rows, LANES), F32),
            VMEM((rows, LANES), F32),
            VMEM((spans, REACH, LANES), F32),
            VMEM((spans, REACH, LANES), F32),
            VMEM((spans, REACH, LANES), F32),
            VMEM((spans, REACH, LANES), F32),
            VMEM((8, LANES), F32),
            VMEM((LANES, LANES), F32),
            VMEM((LANES, LANES), F32),
            VMEM((HALF, spans, LANES), F32),
            VMEM((HALF, spans, LANES), F32),
            VMEM((spans, HALF, LANES), F32),
            VMEM((spans, LANES), F32),
            VMEM((3, 8, 8, LANES), F32),
            VMEM((8, 8, LANES), F32),
            VMEM((dofs, LANES), F32),
            pltpu.SemaphoreType.DMA((15,)),
            pltpu.SemaphoreType.DMA((15,)),
            pltpu.SemaphoreType.DMA((15,)),
        ],
        compiler_params=params(0),
    )(
        current_block[0],
        search_block[0],
        previous_block[0],
        [
            coef.reshape(grid)
            for coef in (ground_spring, wire_tension, dropper_stiff, span_link)
        ],
        dropper_offset.reshape(grid),
        ritz_rotation[0].T,
        jnp.asarray(left_terms(matrix)),
        jnp.asarray(left_terms(matrix.T)),
        slots,
    )
    next_block, next_residual, ritz = pl.pallas_call(
        finish_kernel,
        out_shape=(shape(M, dofs), shape(M, dofs), shape(1, M)),
        in_specs=full(3),
        out_specs=tuple(full(3)),
        scratch_shapes=[VMEM((dofs, LANES), F32)],
        compiler_params=params(limit=60),
    )(block, got, ritz)
    return (next_block[None], next_residual[None], ritz)


def solution(mesh):
    return jax.shard_map(
        on_device,
        mesh=mesh,
        in_specs=(
            P("span", None, "elem"),
            P("span", None, "elem"),
            P("span", None, "elem"),
            P("elem"),
            P("elem"),
            P("elem"),
            P("elem"),
            P("elem"),
            P("span", None, None),
        ),
        out_specs=(P("span", None, "elem"), P("span", None, "elem"), P("span", None)),
        check_vma=False,
    )
```
